32 devices in a mesh: gx: 2 (over core), gy: 16 (over z, y, x).
Axes of the slice: x: 2, y: 2, z: 4, core: 2. Of those that a mesh axis runs over, the one named last changes fastest.
Arguments:
- krylov: float32 [2, 256, 8, 2, 256], P('gx', 'gy'), may hold values from -6 to 6
- block_inverse: float32 [2, 256, 2, 2, 256], P('gx', 'gy'), may hold values from -0.02 to 0.07, as said below
- back_coupling: float32 [2, 256, 2, 2, 256], P('gx', 'gy'), may hold values from -0.3 to 0.06, as said below
- front_coupling: float32 [2, 256, 2, 2, 256], P('gx', 'gy'), may hold values from -0.3 to 0.06, as said below
- left_coupling: float32 [2, 256, 2, 2, 256], P('gx', 'gy'), may hold values from -10240 to 10240, as said below
- right_coupling: float32 [2, 256, 2, 2, 256], P('gx', 'gy'), may hold values from -10240 to 10240, as said below
Outputs:
- preconditioned: float32 [2, 256, 8, 2, 256], P('gx', 'gy')
The draws below stay inside these ranges and needn't reach their ends.
Inputs may be any that keep to these rules, and one draw needn't show every extreme that they name: `block_inverse`: a 2x2 block for each cell. `back_coupling`: a 2x2 block for each cell. `front_coupling`: a 2x2 block for each cell. `left_coupling`: a 2x2 block for each cell. `right_coupling`: a 2x2 block for each cell.
All inputs are finite; a program needn't handle non-finite values.
Results may differ from the reference program's by a relative error of at most 0.00018.
Values sent between devices are 32-bit elements; how exact they have to be, the bound alone decides.
No kernel may reach another device: no remote copies, remote signals or barrier semaphores. Data moves between devices by JAX's collectives and lax.ppermute only.
A program may use at most 64 MiB of HBM per device.

```python
import jax
import jax.numpy as jnp
from jax import lax

KV = 8
NZ = 256
PLANE_TOTAL = 2
LINES_PER_PLANE = 256


def make_block(upper_left, upper_right, lower_left, lower_right):
    upper_row = jnp.stack([upper_left, upper_right], axis=2)
    bottom_block_row = jnp.stack([lower_left, lower_right], axis=2)
    return jnp.stack([upper_row, bottom_block_row], axis=2)


def block_draw(key, stream_id, lowest, highest, spread, polarity):
    folded = jax.random.fold_in(key, stream_id)
    first_key, second_key = jax.random.split(folded)
    diagonal = jnp.exp(jax.random.uniform(first_key, (PLANE_TOTAL, LINES_PER_PLANE, 2, NZ), jnp.float32, jnp.log(lowest), jnp.log(highest)))
    off_diagonal = jax.random.uniform(second_key, (PLANE_TOTAL, LINES_PER_PLANE, 2, NZ), jnp.float32, -spread, spread)
    return make_block(polarity * diagonal[:, :, 0], off_diagonal[:, :, 0], off_diagonal[:, :, 1], polarity * diagonal[:, :, 1])


def decay_length(key):
    folded = jax.random.fold_in(key, 17)
    line_total = 1.0 * LINES_PER_PLANE
    length = jnp.exp(jax.random.uniform(folded, (PLANE_TOTAL, 1, NZ), jnp.float32, jnp.log(30.0), jnp.log(8.0 * line_total)))
    return length


def inverse_entries(key):
    folded = jax.random.fold_in(key, 3)
    first_key, second_key = jax.random.split(folded)
    diagonal = jnp.exp(jax.random.uniform(first_key, (PLANE_TOTAL, LINES_PER_PLANE, 2, NZ), jnp.float32, jnp.log(0.5), jnp.log(1.0)))
    off_diagonal = jax.random.uniform(second_key, (PLANE_TOTAL, LINES_PER_PLANE, 2, NZ), jnp.float32, -0.3, 0.3)
    scale = -2.0 * jnp.expm1(-1.0 / decay_length(key))
    return (scale * diagonal[:, :, 0], scale * off_diagonal[:, :, 0], scale * off_diagonal[:, :, 1], scale * diagonal[:, :, 1])


def line_coupling(key, stream_id, polarity):
    first_diag, upper_off, lower_off, second_diag = inverse_entries(key)
    determinant = first_diag * second_diag - upper_off * lower_off
    inverse_aa = second_diag / determinant
    inverse_ab = -upper_off / determinant
    inverse_ba = -lower_off / determinant
    inverse_bb = first_diag / determinant
    length = decay_length(key)
    folded = jax.random.fold_in(key, stream_id)
    random_key_sequence = jax.random.split(folded, 4)
    multiplier = jnp.exp(jax.random.uniform(random_key_sequence[1], (PLANE_TOTAL, LINES_PER_PLANE, NZ), jnp.float32, jnp.log(0.5), jnp.log(2.0)))
    random_block_sample = jax.random.randint(random_key_sequence[2], (PLANE_TOTAL, LINES_PER_PLANE, 1), 0, 256)
    relaxation_factor = jnp.where(random_block_sample == 0, 0.6, 1.0).astype(jnp.float32)
    line_rate = jnp.exp(-multiplier / length) * relaxation_factor
    rotation_angle = jax.random.uniform(random_key_sequence[3], (PLANE_TOTAL, LINES_PER_PLANE, NZ), jnp.float32, -0.4, 0.4)
    map_aa = line_rate * jnp.cos(rotation_angle)
    map_ab = -line_rate * jnp.sin(rotation_angle)
    map_ba = line_rate * jnp.sin(rotation_angle)
    map_bb = line_rate * jnp.cos(rotation_angle)
    result_aa = polarity * (inverse_aa * map_aa + inverse_ab * map_ba)
    result_ab = polarity * (inverse_aa * map_ab + inverse_ab * map_bb)
    result_ba = polarity * (inverse_ba * map_aa + inverse_bb * map_ba)
    result_bb = polarity * (inverse_ba * map_ab + inverse_bb * map_bb)
    return make_block(result_aa, result_ab, result_ba, result_bb)


def draw_block_inverse(key, part):
    return make_block(*inverse_entries(key))


def draw_back_coupling(key, part):
    return block_draw(key, 5, 0.1, 0.3, 0.06, -1.0)


def draw_front_coupling(key, part):
    return block_draw(key, 7, 0.1, 0.3, 0.06, -1.0)


def draw_left_coupling(key, part):
    return line_coupling(key, 11, 1.0)


def draw_right_coupling(key, part):
    return line_coupling(key, 13, -1.0)


def shard_levels(rng, shape, cuts, low, top_value):
    def one(position, shards_of):
        heights = jax.random.uniform(jax.random.fold_in(jax.random.fold_in(rng, 6), position), (shards_of,), jnp.float32, low / len(cuts), top_value / len(cuts))
        return jnp.repeat(jnp.exp(heights), shape[position] // shards_of).reshape((-1,) + (1,) * (len(shape) - position - 1))

    factor_of = one(*cuts[0])
    for cut in cuts[1:]:
        factor_of = factor_of * one(*cut)
    return factor_of


def centred(rng, shape, scale, limit, cuts=(), kind=jnp.bfloat16):
    level = shard_levels(rng, shape, cuts, -0.22, 0.18) if cuts else 1.0
    entries = jax.random.normal(rng, shape, jnp.float32) * scale * level
    return jnp.minimum(jnp.maximum(entries, -limit), limit).astype(kind)


def setup_inputs(seed: int = 0) -> dict:
    streams_of = jax.random.split(jax.random.key(seed), 7)
    krylov = centred(streams_of[0], (PLANE_TOTAL, LINES_PER_PLANE, KV, 2, NZ), 1.0, 6.0, ((0, 2), (1, 16)), jnp.float32)
    block_inverse = draw_block_inverse(jax.random.fold_in(streams_of[6], 71), 0)
    back_coupling = draw_back_coupling(jax.random.fold_in(streams_of[6], 71), 0)
    front_coupling = draw_front_coupling(jax.random.fold_in(streams_of[6], 71), 0)
    left_coupling = draw_left_coupling(jax.random.fold_in(streams_of[6], 71), 0)
    right_coupling = draw_right_coupling(jax.random.fold_in(streams_of[6], 71), 0)
    return {"krylov": krylov, "block_inverse": block_inverse, "back_coupling": back_coupling, "front_coupling": front_coupling, "left_coupling": left_coupling, "right_coupling": right_coupling}


def apply_block(matrix, vector):
    spread_matrix = matrix[..., None, :, :, :]
    return spread_matrix[..., 0, :] * vector[..., 0:1, :] + spread_matrix[..., 1, :] * vector[..., 1:2, :]


def solve_plane(source, inverse, left_side, right_side):
    def forward_line(previous, inputs):
        line_source, line_inverse, line_left = inputs
        state_now = apply_block(line_inverse, line_source - apply_block(line_left, previous))
        return state_now, state_now

    start_state = jnp.zeros(source.shape[1:], jnp.float32)
    _, forward_state = lax.scan(forward_line, start_state, (source, inverse, left_side))

    def reverse_line_sweep(following, inputs):
        line_state, line_inverse, line_right = inputs
        state_now = line_state - apply_block(line_inverse, apply_block(line_right, following))
        return state_now, state_now

    _, backward_state = lax.scan(reverse_line_sweep, start_state, (forward_state, inverse, right_side), reverse=True)
    return backward_state


def reference(krylov, block_inverse, back_coupling, front_coupling, left_coupling, right_coupling):
    empty_plane = jnp.zeros((LINES_PER_PLANE, KV, 2, NZ), jnp.float32)

    def forward_plane(previous, inputs):
        source, inverse, back_side, left_side, right_side = inputs
        swept = solve_plane(source - apply_block(back_side, previous), inverse, left_side, right_side)
        return swept, swept

    _, swept_all = lax.scan(forward_plane, empty_plane, (krylov, block_inverse, back_coupling, left_coupling, right_coupling))

    def backward_plane(following, inputs):
        swept, inverse, front_side, left_side, right_side = inputs
        result_plane = swept - solve_plane(apply_block(front_side, following), inverse, left_side, right_side)
        return result_plane, result_plane

    _, preconditioned = lax.scan(backward_plane, empty_plane, (swept_all, block_inverse, front_coupling, left_coupling, right_coupling), reverse=True)
    return preconditioned
```

```python
import functools

import jax
import jax.numpy as jnp
from jax import lax
from jax.experimental import pallas as pl
from jax.experimental.pallas import tpu as pltpu
from jax.sharding import PartitionSpec as P

CHAINS = ((0, 0), (1, 0), (0, 1), (1, 1), (0, 2), (1, 2))
T1, U1, T2, U2, T3, U3 = range(6)
UNITS = 4
VMEM = pl.BlockSpec(memory_space=pltpu.VMEM)
ANY = pl.BlockSpec(memory_space=pl.ANY)
HBM = pl.BlockSpec(memory_space=pltpu.HBM)


def spot(chain):
    direction, number = CHAINS[chain]
    return 3 * direction + number


def feeds(chain):
    return range(min(chain + 1, UNITS))


def spread(ref, row, count):
    return ref[pl.ds(row, count, stride=0), :]


def call(kernel, name, outs, ins, scratch=(), specs=None, out_specs=None):
    return pl.pallas_call(
        kernel,
        name=name,
        out_shape=[jax.ShapeDtypeStruct(s, jnp.float32) for s in outs],
        in_specs=specs or [VMEM] * len(ins),
        out_specs=out_specs or [VMEM] * len(outs),
        scratch_shapes=list(scratch),
        compiler_params=pltpu.CompilerParams(vmem_limit_bytes=8 << 20),
    )(*ins)


def pack_kernel(half, vectors, krylov, inverse, back, front, left, right, keep, send, sems):
    core = lax.axis_index("gx")
    base = (0, vectors, vectors + 2, vectors + 4, vectors + 6)

    def copies(ref, position, target, number):
        lanes = pl.ds(pl.multiple_of(position * half, half), half)
        size = ref.shape[2]
        return pltpu.make_async_copy(
            ref.at[0, :, :, :, lanes],
            target.at[:, pl.ds(base[number], size)],
            sems.at[number, 0 if target is keep else 1],
        )

    fixed = (krylov, inverse, left, right)
    plan = [
        copies(ref, position, target, number)
        for target, position in ((send, 1 - core), (keep, core))
        for number, ref in enumerate(fixed)
    ]
    for copy in plan:
        copy.start()
    for own, ref in ((0, front), (1, back)):

        @pl.when(core == own)
        def _():
            pair = [copies(ref, 1 - core, send, 4), copies(ref, core, keep, 4)]
            for copy in pair:
                copy.start()
            for copy in pair:
                copy.wait()

    for copy in plan:
        copy.wait()


def local_kernel(lines, vectors, keep, recv, edge, first, second, low, data, maps):
    core = lax.axis_index("gx")
    pitch = 2 * vectors + 16
    rows = lines * pitch
    width = vectors + 2 * UNITS
    mine, other = keep[...], recv[...]
    data[pl.ds(0, rows), :] = jnp.where(core == 0, mine, other)
    data[pl.ds(rows, rows), :] = jnp.where(core == 0, other, mine)

    def block(plane, number):
        start = plane * rows + 2 * vectors + 4 * number
        return [[data[pl.ds(start + 2 * a + b, lines, stride=pitch), :] for b in (0, 1)] for a in (0, 1)]

    def keep_map(number, left, right):
        for a in (0, 1):
            for b in (0, 1):
                value = -(left[a][0] * right[0][b] + left[a][1] * right[1][b])
                maps[pl.ds((4 * number + 2 * a + b) * lines, lines), :] = value

    for plane in (0, 1):
        inverse = block(plane, 0)
        keep_map(2 * plane, inverse, block(plane, 1))
        keep_map(2 * plane + 1, inverse, block(plane, 2))
        keep_map(4 + plane, inverse, block(plane, 3))

    def product(ref, place, state):
        out = []
        for a in (0, 1):
            left, right = (spread(ref, place(a, b), 8) for b in (0, 1))
            out.append([left * x + right * y for x, y in zip(state[0], state[1])])
        return out

    def mapped(number, line, state):
        return product(maps, lambda a, b: (4 * number + 2 * a + b) * lines + line, state)

    def add(x, y):
        return [[p + q for p, q in zip(s, t)] for s, t in zip(x, y)]

    row = lax.broadcasted_iota(jnp.int32, (8, 128), 0)
    none = jnp.zeros((8, 128), jnp.float32)

    def unit(chain):
        one = [jnp.where(row == 2 * chain + a, 1.0, 0.0) for a in (0, 1)] if chain < UNITS else [none, none]
        return [[none, one[a]] for a in (0, 1)]

    def scaled(plane, line):
        start = plane * rows + line * pitch
        source = [[data[pl.ds(start + a, vectors, stride=2), :]] for a in (0, 1)]
        got = product(data, lambda a, b: start + 2 * vectors + 2 * a + b, source)
        return [[s[0], none] for s in got]

    def leave(chain, state):
        for a in (0, 1):
            for half in (0, 1):
                edge[pl.ds((2 * spot(chain) + a) * width + half * 8, 8), :] = state[a][half]

    def solve(plane, chain, source):
        state, states = unit(chain), []
        for line in range(lines):
            state = add(source(line), mapped(2 * plane, line, state))
            states.append(state)
        leave(chain, state)
        state, result = unit(chain + 1), [None] * lines
        for line in reversed(range(lines)):
            state = add(states[line], mapped(2 * plane + 1, line, state))
            result[line] = state
        leave(chain + 1, state)
        return result

    swept_low = solve(0, T1, lambda line: scaled(0, line))
    for line in range(lines):
        for a in (0, 1):
            low[pl.ds((2 * line + a) * 8, 8), :] = swept_low[line][a][1]
    swept_high = solve(1, T2, lambda line: add(scaled(1, line), mapped(5, line, swept_low[line])))
    fixed = solve(0, T3, lambda line: mapped(4, line, swept_high[line]))
    for line in range(lines):
        total = add(swept_low[line], fixed[line])
        for a in (0, 1):
            for half in (0, 1):
                place = pl.ds((2 * line + a) * width + half * 8, 8)
                first[place, :] = total[a][half]
                second[place, :] = swept_high[line][a][half]


def response(ref, width, to, frm, state, start=0):
    if frm >= UNITS:
        to, frm = to - UNITS, frm - UNITS
    out = []
    for a in (0, 1):
        row = (2 * (spot(to) - start) + a) * width + width - 2 * UNITS + 2 * frm
        left, right = spread(ref, row, 8), spread(ref, row + 1, 8)
        out.append([left * x + right * y for x, y in zip(state[0], state[1])])
    return out


def total(first, *others):
    for other in others:
        first = [[p + q for p, q in zip(s, t)] for s, t in zip(first, other)]
    return first


def merge_kernel(bit, width, last, mine, other, edge, mids, lower, upper):
    is_low = jnp.bitwise_and(lax.axis_index("gy"), bit) == 0
    x, y = mine[...], other[...]
    lower[...] = jnp.where(is_low, x, y)
    upper[...] = jnp.where(is_low, y, x)
    row = lax.broadcasted_iota(jnp.int32, (8, 128), 0)
    up = jnp.bitwise_and(row, 2) == 0

    def base(ref, chain, keep_up):
        out = []
        for a in (0, 1):
            start = (2 * spot(chain) + a) * width
            units = ref[pl.ds(start + 8, 8), :]
            out.append([ref[pl.ds(start, 8), :], jnp.where(up if keep_up else ~up, units, 0.0)])
        return out

    low = functools.partial(response, lower, width)
    high = functools.partial(response, upper, width)
    m = [None] * 6
    m[T1] = base(lower, T1, True)
    m[U1] = total(base(upper, U1, False), high(U1, T1, m[T1]))
    m[T2] = total(base(lower, T2, True), low(T2, U1, m[U1]))
    m[U2] = total(base(upper, U2, False), high(U2, T1, m[T1]), high(U2, T2, m[T2]))
    m[T3] = total(base(lower, T3, True), low(T3, U1, m[U1]), low(T3, U2, m[U2]))
    m[U3] = total(base(upper, U3, False), high(U3, T1, m[T1]), high(U3, T2, m[T2]), high(U3, T3, m[T3]))
    e = [None] * 6
    for chain in range(6):
        ref, of = (upper, high) if CHAINS[chain][0] == 0 else (lower, low)
        through = [c for c in range(chain + 1) if CHAINS[c][0] == CHAINS[chain][0]]
        e[chain] = total(base(ref, chain, CHAINS[chain][0] == 1), *(of(chain, c, m[c]) for c in through))
    next_low = jnp.bitwise_and(lax.axis_index("gy"), 2 * bit) == 0
    for chain in range(6):
        for a in (0, 1):
            for half in (0, 1):
                place = (2 * spot(chain) + a) * width + 8 * half
                mids[pl.ds(place, 8), :] = m[chain][a][half]
                if not last:
                    edge[pl.ds(place, 8), :] = e[chain][a][half]
                elif chain % 2 == 0:
                    edge[pl.ds(place, 8), :] = jnp.where(next_low, e[chain][a][half], e[chain + 1][a][half])


def finish_kernel(lines, levels, width, mine, other, *refs):
    mids, (first, second, low, kept, sent, ups, downs) = refs[: levels - 1], refs[levels - 1 :]
    core, place = lax.axis_index("gx"), lax.axis_index("gy")
    is_low = jnp.bitwise_and(place, 1 << (levels - 1)) == 0
    x, y = mine[...], other[...]
    ups[...] = jnp.where(is_low, x, y)
    downs[...] = jnp.where(is_low, y, x)

    def base(ref, chain, start):
        return [[ref[pl.ds((2 * (spot(chain) - start) + a) * width, 8), :]] for a in (0, 1)]

    def up(to, frm, state):
        return response(ups, width, to, frm, state)

    def down(to, frm, state):
        return response(downs, width, to, frm, state, 3)

    m = [None] * 6
    m[T1] = base(ups, T1, 0)
    m[U1] = total(base(downs, U1, 3), down(U1, T1, m[T1]))
    m[T2] = total(base(ups, T2, 0), up(T2, U1, m[U1]))
    m[U2] = total(base(downs, U2, 3), down(U2, T1, m[T1]), down(U2, T2, m[T2]))
    m[T3] = total(base(ups, T3, 0), up(T3, U1, m[U1]), up(T3, U2, m[U2]))
    m[U3] = total(base(downs, U3, 3), down(U3, T1, m[T1]), down(U3, T2, m[T2]), down(U3, T3, m[T3]))

    def select(condition, x, y):
        return [[jnp.where(condition, p, q) for p, q in zip(s, t)] for s, t in zip(x, y)]

    none = [[jnp.zeros((8, 128), jnp.float32)], [jnp.zeros((8, 128), jnp.float32)]]
    enters = [none] * 6
    for level in reversed(range(levels)):
        if level < levels - 1:
            ref = mids[level]
            m = []
            for chain in range(6):
                terms = [response(ref, width, chain, c, enters[c]) for c in feeds(chain)]
                if chain >= UNITS:
                    terms += [response(ref, width, chain, c, enters[c]) for c in range(UNITS, chain + 1)]
                m.append(total(base(ref, chain, 0), *terms))
        is_low = jnp.bitwise_and(place, 1 << level) == 0
        enters = [
            select(is_low, enters[c], m[c]) if CHAINS[c][0] == 0 else select(is_low, m[c], enters[c])
            for c in range(6)
        ]

    def columns(ref, start, chains):
        value = None
        for place_of, chain in chains:
            for b in (0, 1):
                term = spread(ref, start + 2 * place_of + b, 8) * enters[chain][b][0]
                value = term if value is None else value + term
        return value

    for line in range(lines):
        for a in (0, 1):
            start = (2 * line + a) * width
            units = [(c, c) for c in range(UNITS)]
            high = second[pl.ds(start, 8), :] + columns(second, start + 8, units)
            own = first[pl.ds(start, 8), :] + columns(first, start + 8, units)
            own = own + columns(low, (2 * line + a) * 8, [(T1, T3), (U1, U3)])
            target = pl.ds(line * 16 + a, 8, stride=2)
            kept[target, :] = jnp.where(core == 0, own, high)
            sent[target, :] = jnp.where(core == 0, high, own)


def unpack_kernel(half, kept, got, out, sems):
    core = lax.axis_index("gx")
    plan = []
    for number, (ref, position) in enumerate(((kept, core), (got, 1 - core))):
        lanes = pl.ds(pl.multiple_of(position * half, half), half)
        plan.append(pltpu.make_async_copy(ref, out.at[0, :, :, :, lanes], sems.at[number]))
    for copy in plan:
        copy.start()
    for copy in plan:
        copy.wait()


def per_device(krylov, inverse, back, front, left, right):
    _, lines, vectors, _, cells = krylov.shape
    count = lax.axis_size("gy")
    levels = count.bit_length() - 1
    half = cells // 2
    width = vectors + 2 * UNITS
    assert lax.axis_size("gx") == 2 and count == 1 << levels and levels > 1
    assert vectors == 8 and half == 128
    swap = [(0, 1), (1, 0)]

    slots = vectors + 8
    keep, send = call(
        functools.partial(pack_kernel, half, vectors),
        "pack",
        [(lines, slots, 2, half)] * 2,
        [pltpu.with_memory_space_constraint(x, pltpu.HBM) for x in (krylov, inverse, back, front, left, right)],
        [pltpu.SemaphoreType.DMA((5, 2))],
        specs=[HBM] * 6,
    )
    recv = lax.ppermute(send.reshape(-1, half), "gx", swap)
    keep = keep.reshape(-1, half)
    edge, first, second, low = call(
        functools.partial(local_kernel, lines, vectors),
        "local",
        [(12 * width, half), (2 * lines * width, half), (2 * lines * width, half), (2 * lines * 8, half)],
        (keep, recv),
        [pltpu.VMEM((2 * keep.shape[0], half), jnp.float32), pltpu.VMEM((24 * lines, half), jnp.float32)],
    )
    mids = []
    for level in range(levels - 1):
        got = lax.ppermute(edge, "gy", [(j, j ^ (1 << level)) for j in range(count)])
        last = level == levels - 2
        edge, mid = call(
            functools.partial(merge_kernel, 1 << level, width, last),
            f"merge{level}",
            [((6 if last else 12) * width, half), (12 * width, half)],
            (edge, got),
            [pltpu.VMEM((12 * width, half), jnp.float32)] * 2,
        )
        mids.append(mid)
    got = lax.ppermute(edge, "gy", [(j, j ^ (count // 2)) for j in range(count)])
    kept, sent = call(
        functools.partial(finish_kernel, lines, levels, width),
        "finish",
        [(lines * 16, half)] * 2,
        (edge, got, *mids, first, second, low),
        [pltpu.VMEM((6 * width, half), jnp.float32)] * 2,
    )
    got = lax.ppermute(sent, "gx", swap)
    (out,) = call(
        functools.partial(unpack_kernel, half),
        "unpack",
        [krylov.shape],
        [x.reshape(lines, vectors, 2, half) for x in (kept, got)],
        [pltpu.SemaphoreType.DMA((2,))],
        specs=[ANY] * 2,
        out_specs=[HBM],
    )
    return out


def solution(mesh):
    spec = P("gx", "gy", None, None, None)
    return jax.shard_map(
        per_device, mesh=mesh, in_specs=(spec,) * 6, out_specs=spec, check_vma=False
    )
```

```python
import functools

import jax
import jax.numpy as jnp
from jax import lax
from jax.experimental import pallas as pl
from jax.experimental.pallas import tpu as pltpu
from jax.sharding import PartitionSpec as P

CHAINS = ((0, 0), (1, 0), (0, 1), (1, 1), (0, 2), (1, 2))
T1, U1, T2, U2, T3, U3 = range(6)
UNITS = 4
VMEM = pl.BlockSpec(memory_space=pltpu.VMEM)
ANY = pl.BlockSpec(memory_space=pl.ANY)
HBM = pl.BlockSpec(memory_space=pltpu.HBM)


def spot(chain):
    direction, number = CHAINS[chain]
    return 3 * direction + number


def feeds(chain):
    return range(min(chain + 1, UNITS))


UNIT_START = {U1: (0, 4), T2: (8, 8), T1: (14, 8), U2: (24, 8), T3: (40, 8), U3: (56, 8)}
VECTOR_ROWS = 96
ROWS = VECTOR_ROWS + 72
UP_ROWS = {(T2, U1): (0, 2), (T3, U1): (4, 4), (T3, U2): (6, 4)}
DOWN_ROWS = {(U1, T1): (0, 2), (U2, T1): (4, 4), (U2, T2): (6, 4), (U3, T1): (12, 4), (U3, T2): (14, 4)}
LAST_UNITS = 24
LAST_ROWS = VECTOR_ROWS // 2 + LAST_UNITS


def vector_row(chain, a):
    return (2 * spot(chain) + a) * 8


def unit_row(chain, a):
    start, step = UNIT_START[chain]
    return VECTOR_ROWS + start + step * a


def unit_count(chain):
    return 2 * len(feeds(chain))


def half_of():
    top = lax.axis_size("gy") // 2
    flip = jnp.where(jnp.bitwise_and(lax.axis_index("gy"), top) == 0, 0, 1)
    return jnp.bitwise_xor(lax.axis_index("gx"), flip)


def keep_record(ref, values):
    for chain in range(6):
        for a in (0, 1):
            carries, units = values[chain][a]
            ref[pl.ds(vector_row(chain, a), 8), :] = carries
            count = unit_count(chain)
            ref[pl.ds(unit_row(chain, a), count), :] = units[:count]


def spread(ref, row, count):
    return ref[pl.ds(row, count, stride=0), :]


def call(kernel, name, outs, ins, scratch=(), specs=None, out_specs=None):
    return pl.pallas_call(
        kernel,
        name=name,
        out_shape=[jax.ShapeDtypeStruct(s, jnp.float32) for s in outs],
        in_specs=specs or [VMEM] * len(ins),
        out_specs=out_specs or [VMEM] * len(outs),
        scratch_shapes=list(scratch),
        compiler_params=pltpu.CompilerParams(vmem_limit_bytes=8 << 20),
    )(*ins)


def pack_kernel(half, vectors, krylov, inverse, back, front, left, right, keep, send, sems):
    core, part = lax.axis_index("gx"), half_of()
    base = (0, vectors, vectors + 2, vectors + 4, vectors + 6)

    def copies(ref, position, target, number):
        lanes = pl.ds(pl.multiple_of(position * half, half), half)
        size = ref.shape[2]
        return pltpu.make_async_copy(
            ref.at[0, :, :, :, lanes],
            target.at[:, pl.ds(base[number], size)],
            sems.at[number, 0 if target is keep else 1],
        )

    fixed = (krylov, inverse, left, right)
    plan = [
        copies(ref, position, target, number)
        for target, position in ((send, 1 - part), (keep, part))
        for number, ref in enumerate(fixed)
    ]
    for copy in plan:
        copy.start()
    for own, ref in ((0, front), (1, back)):

        @pl.when(core == own)
        def _():
            pair = [copies(ref, 1 - part, send, 4), copies(ref, part, keep, 4)]
            for copy in pair:
                copy.start()
            for copy in pair:
                copy.wait()

    for copy in plan:
        copy.wait()


def local_kernel(lines, vectors, keep, recv, edge, first, second, low, data, maps):
    core = lax.axis_index("gx")
    pitch = 2 * vectors + 16
    rows = lines * pitch
    width = vectors + 2 * UNITS
    mine, other = keep[...], recv[...]
    data[pl.ds(0, rows), :] = jnp.where(core == 0, mine, other)
    data[pl.ds(rows, rows), :] = jnp.where(core == 0, other, mine)

    def block(plane, number):
        start = plane * rows + 2 * vectors + 4 * number
        return [[data[pl.ds(start + 2 * a + b, lines, stride=pitch), :] for b in (0, 1)] for a in (0, 1)]

    def keep_map(number, left, right):
        for a in (0, 1):
            for b in (0, 1):
                value = -(left[a][0] * right[0][b] + left[a][1] * right[1][b])
                maps[pl.ds((4 * number + 2 * a + b) * lines, lines), :] = value

    for plane in (0, 1):
        inverse = block(plane, 0)
        keep_map(2 * plane, inverse, block(plane, 1))
        keep_map(2 * plane + 1, inverse, block(plane, 2))
        keep_map(4 + plane, inverse, block(plane, 3))

    def product(ref, place, state):
        out = []
        for a in (0, 1):
            left, right = (spread(ref, place(a, b), 8) for b in (0, 1))
            out.append([left * x + right * y for x, y in zip(state[0], state[1])])
        return out

    def mapped(number, line, state):
        return product(maps, lambda a, b: (4 * number + 2 * a + b) * lines + line, state)

    def add(x, y):
        return [[p + q for p, q in zip(s, t)] for s, t in zip(x, y)]

    row = lax.broadcasted_iota(jnp.int32, (8, 128), 0)
    none = jnp.zeros((8, 128), jnp.float32)

    def unit(chain):
        one = [jnp.where(row == 2 * chain + a, 1.0, 0.0) for a in (0, 1)] if chain < UNITS else [none, none]
        return [[none, one[a]] for a in (0, 1)]

    def scaled(plane, line):
        start = plane * rows + line * pitch
        source = [[data[pl.ds(start + a, vectors, stride=2), :]] for a in (0, 1)]
        got = product(data, lambda a, b: start + 2 * vectors + 2 * a + b, source)
        return [[s[0], none] for s in got]

    leaving = [None] * 6

    def solve(plane, chain, source):
        state, states = unit(chain), []
        for line in range(lines):
            state = add(source(line), mapped(2 * plane, line, state))
            states.append(state)
        leaving[chain] = state
        state, result = unit(chain + 1), [None] * lines
        for line in reversed(range(lines)):
            state = add(states[line], mapped(2 * plane + 1, line, state))
            result[line] = state
        leaving[chain + 1] = state
        return result

    swept_low = solve(0, T1, lambda line: scaled(0, line))
    for line in range(lines):
        for a in (0, 1):
            low[pl.ds((2 * line + a) * 8, 8), :] = swept_low[line][a][1]
    swept_high = solve(1, T2, lambda line: add(scaled(1, line), mapped(5, line, swept_low[line])))
    fixed = solve(0, T3, lambda line: mapped(4, line, swept_high[line]))
    keep_record(edge, leaving)
    for line in range(lines):
        total = add(swept_low[line], fixed[line])
        for a in (0, 1):
            for half in (0, 1):
                place = pl.ds((2 * line + a) * width + half * 8, 8)
                first[place, :] = total[a][half]
                second[place, :] = swept_high[line][a][half]


def times(ref, row, step, state):
    out = []
    for a in (0, 1):
        left, right = spread(ref, row + step * a, 8), spread(ref, row + step * a + 1, 8)
        out.append([left * x + right * y for x, y in zip(state[0], state[1])])
    return out


def response(ref, to, frm, state):
    if frm >= UNITS:
        to, frm = to - UNITS, frm - UNITS
    start, step = UNIT_START[to]
    return times(ref, VECTOR_ROWS + start + 2 * frm, step, state)


def total(first, *others):
    for other in others:
        first = [[p + q for p, q in zip(s, t)] for s, t in zip(first, other)]
    return first


def merge_kernel(bit, last, mine, other, edge, mids, lower, upper, *pair):
    is_low = jnp.bitwise_and(lax.axis_index("gy"), bit) == 0
    x, y = mine[...], other[...]
    lower[...] = jnp.where(is_low, x, y)
    upper[...] = jnp.where(is_low, y, x)
    row = lax.broadcasted_iota(jnp.int32, (8, 128), 0)
    up = jnp.bitwise_and(row, 2) == 0

    def base(ref, chain, keep_up):
        wanted = (up if keep_up else ~up) & (row < unit_count(chain))
        out = []
        for a in (0, 1):
            units = ref[pl.ds(unit_row(chain, a), 8), :]
            out.append([ref[pl.ds(vector_row(chain, a), 8), :], jnp.where(wanted, units, 0.0)])
        return out

    low = functools.partial(response, lower)
    high = functools.partial(response, upper)
    m = [None] * 6
    m[T1] = base(lower, T1, True)
    m[U1] = total(base(upper, U1, False), high(U1, T1, m[T1]))
    m[T2] = total(base(lower, T2, True), low(T2, U1, m[U1]))
    m[U2] = total(base(upper, U2, False), high(U2, T1, m[T1]), high(U2, T2, m[T2]))
    m[T3] = total(base(lower, T3, True), low(T3, U1, m[U1]), low(T3, U2, m[U2]))
    m[U3] = total(base(upper, U3, False), high(U3, T1, m[T1]), high(U3, T2, m[T2]), high(U3, T3, m[T3]))
    e = [None] * 6
    for chain in range(6):
        ref, of = (upper, high) if CHAINS[chain][0] == 0 else (lower, low)
        through = [c for c in range(chain + 1) if CHAINS[c][0] == CHAINS[chain][0]]
        e[chain] = total(base(ref, chain, CHAINS[chain][0] == 1), *(of(chain, c, m[c]) for c in through))
    keep_record(mids, m)
    if not last:
        keep_record(edge, e)
        return
    next_low = jnp.bitwise_and(lax.axis_index("gy"), 2 * bit) == 0
    for chain in (T1, T2, T3):
        for a in (0, 1):
            place = pl.ds(vector_row(chain, a), 8)
            edge[place, :] = jnp.where(next_low, e[chain][a][0], e[chain + 1][a][0])
    for ref, table in zip(pair, (UP_ROWS, DOWN_ROWS)):
        ref[...] = jnp.zeros_like(ref)
        for (to, frm), (start, step) in table.items():
            for a in (0, 1):
                ref[pl.ds(start + step * a, 2), :] = e[to][a][1][2 * frm : 2 * frm + 2]
    units = pl.ds(VECTOR_ROWS // 2, LAST_UNITS)
    edge[units, :] = jnp.where(next_low, pair[0][...], pair[1][...])


def finish_kernel(lines, levels, mine, other, *refs):
    mids, (first, second, low, kept, sent, ups, downs) = refs[: levels - 1], refs[levels - 1 :]
    core, place = lax.axis_index("gx"), lax.axis_index("gy")
    is_low = jnp.bitwise_and(place, 1 << (levels - 1)) == 0
    x, y = mine[...], other[...]
    ups[...] = jnp.where(is_low, x, y)
    downs[...] = jnp.where(is_low, y, x)

    width = 8 + 2 * UNITS

    def base(ref, chain, first_chain):
        skip = vector_row(first_chain, 0)
        return [[ref[pl.ds(vector_row(chain, a) - skip, 8), :]] for a in (0, 1)]

    def up(to, frm, state):
        start, step = UP_ROWS[to, frm]
        return times(ups, VECTOR_ROWS // 2 + start, step, state)

    def down(to, frm, state):
        if frm >= UNITS:
            to, frm = to - UNITS, frm - UNITS
        start, step = DOWN_ROWS[to, frm]
        return times(downs, VECTOR_ROWS // 2 + start, step, state)

    m = [None] * 6
    m[T1] = base(ups, T1, T1)
    m[U1] = total(base(downs, U1, U1), down(U1, T1, m[T1]))
    m[T2] = total(base(ups, T2, T1), up(T2, U1, m[U1]))
    m[U2] = total(base(downs, U2, U1), down(U2, T1, m[T1]), down(U2, T2, m[T2]))
    m[T3] = total(base(ups, T3, T1), up(T3, U1, m[U1]), up(T3, U2, m[U2]))
    m[U3] = total(base(downs, U3, U1), down(U3, T1, m[T1]), down(U3, T2, m[T2]), down(U3, T3, m[T3]))

    def select(condition, x, y):
        return [[jnp.where(condition, p, q) for p, q in zip(s, t)] for s, t in zip(x, y)]

    none = [[jnp.zeros((8, 128), jnp.float32)], [jnp.zeros((8, 128), jnp.float32)]]
    enters = [none] * 6
    for level in reversed(range(levels)):
        if level < levels - 1:
            ref = mids[level]
            m = []
            for chain in range(6):
                terms = [response(ref, chain, c, enters[c]) for c in feeds(chain)]
                if chain >= UNITS:
                    terms += [response(ref, chain, c, enters[c]) for c in range(UNITS, chain + 1)]
                m.append(total(base(ref, chain, T1), *terms))
        is_low = jnp.bitwise_and(place, 1 << level) == 0
        enters = [
            select(is_low, enters[c], m[c]) if CHAINS[c][0] == 0 else select(is_low, m[c], enters[c])
            for c in range(6)
        ]

    def columns(ref, start, chains):
        value = None
        for place_of, chain in chains:
            for b in (0, 1):
                term = spread(ref, start + 2 * place_of + b, 8) * enters[chain][b][0]
                value = term if value is None else value + term
        return value

    for line in range(lines):
        for a in (0, 1):
            start = (2 * line + a) * width
            units = [(c, c) for c in range(UNITS)]
            high = second[pl.ds(start, 8), :] + columns(second, start + 8, units)
            own = first[pl.ds(start, 8), :] + columns(first, start + 8, units)
            own = own + columns(low, (2 * line + a) * 8, [(T1, T3), (U1, U3)])
            target = pl.ds(line * 16 + a, 8, stride=2)
            kept[target, :] = jnp.where(core == 0, own, high)
            sent[target, :] = jnp.where(core == 0, high, own)


def unpack_kernel(half, kept, got, out, sems):
    part = half_of()
    plan = []
    for number, (ref, position) in enumerate(((kept, part), (got, 1 - part))):
        lanes = pl.ds(pl.multiple_of(position * half, half), half)
        plan.append(pltpu.make_async_copy(ref, out.at[0, :, :, :, lanes], sems.at[number]))
    for copy in plan:
        copy.start()
    for copy in plan:
        copy.wait()


def per_device(krylov, inverse, back, front, left, right):
    _, lines, vectors, _, cells = krylov.shape
    count = lax.axis_size("gy")
    levels = count.bit_length() - 1
    half = cells // 2
    width = vectors + 2 * UNITS
    assert lax.axis_size("gx") == 2 and count == 1 << levels and levels > 1
    assert vectors == 8 and half == 128
    swap = [(0, 1), (1, 0)]

    slots = vectors + 8
    keep, send = call(
        functools.partial(pack_kernel, half, vectors),
        "pack",
        [(lines, slots, 2, half)] * 2,
        [pltpu.with_memory_space_constraint(x, pltpu.HBM) for x in (krylov, inverse, back, front, left, right)],
        [pltpu.SemaphoreType.DMA((5, 2))],
        specs=[HBM] * 6,
    )
    recv = lax.ppermute(send.reshape(-1, half), "gx", swap)
    keep = keep.reshape(-1, half)
    edge, first, second, low = call(
        functools.partial(local_kernel, lines, vectors),
        "local",
        [(ROWS, half), (2 * lines * width, half), (2 * lines * width, half), (2 * lines * 8, half)],
        (keep, recv),
        [pltpu.VMEM((2 * keep.shape[0], half), jnp.float32), pltpu.VMEM((24 * lines, half), jnp.float32)],
    )
    mids = []
    for level in range(levels - 1):
        got = lax.ppermute(edge, "gy", [(j, j ^ (1 << level)) for j in range(count)])
        last = level == levels - 2
        edge, mid = call(
            functools.partial(merge_kernel, 1 << level, last),
            f"merge{level}",
            [(LAST_ROWS if last else ROWS, half), (ROWS, half)],
            (edge, got),
            [pltpu.VMEM((ROWS, half), jnp.float32)] * 2 + [pltpu.VMEM((LAST_UNITS, half), jnp.float32)] * (2 * last),
        )
        mids.append(mid)
    across = [(core * count + j, (1 - core) * count + (j ^ (count // 2))) for core in (0, 1) for j in range(count)]
    got = lax.ppermute(edge, ("gx", "gy"), across)
    kept, sent = call(
        functools.partial(finish_kernel, lines, levels),
        "finish",
        [(lines * 16, half)] * 2,
        (edge, got, *mids, first, second, low),
        [pltpu.VMEM((LAST_ROWS, half), jnp.float32)] * 2,
    )
    got = lax.ppermute(sent, "gx", swap)
    (out,) = call(
        functools.partial(unpack_kernel, half),
        "unpack",
        [krylov.shape],
        [x.reshape(lines, vectors, 2, half) for x in (kept, got)],
        [pltpu.SemaphoreType.DMA((2,))],
        specs=[ANY] * 2,
        out_specs=[HBM],
    )
    return out


def solution(mesh):
    spec = P("gx", "gy", None, None, None)
    return jax.shard_map(
        per_device, mesh=mesh, in_specs=(spec,) * 6, out_specs=spec, check_vma=False
    )
```

```python
import functools

import jax
import jax.numpy as jnp
from jax import lax
from jax.experimental import pallas as pl
from jax.experimental.pallas import tpu as pltpu
from jax.sharding import PartitionSpec as P

CHAINS = ((0, 0), (1, 0), (0, 1), (1, 1), (0, 2), (1, 2))
T1, U1, T2, U2, T3, U3 = range(6)
UNITS = 4
VMEM = pl.BlockSpec(memory_space=pltpu.VMEM)
ANY = pl.BlockSpec(memory_space=pl.ANY)
HBM = pl.BlockSpec(memory_space=pltpu.HBM)


def spot(chain):
    direction, number = CHAINS[chain]
    return 3 * direction + number


def feeds(chain):
    return range(min(chain + 1, UNITS))


UNIT_START = {U1: (0, 4), T2: (8, 8), T1: (14, 8), U2: (24, 8), T3: (40, 8), U3: (56, 8)}
VECTOR_ROWS = 96
ROWS = VECTOR_ROWS + 72
UP_ROWS = {(T2, U1): (0, 2), (T3, U1): (4, 4), (T3, U2): (6, 4)}
DOWN_ROWS = {(U1, T1): (0, 2), (U2, T1): (4, 4), (U2, T2): (6, 4), (U3, T1): (12, 4), (U3, T2): (14, 4)}
LAST_UNITS = 24
LAST_ROWS = VECTOR_ROWS // 2 + LAST_UNITS


def vector_row(chain, a):
    return (2 * spot(chain) + a) * 8


def unit_row(chain, a):
    start, step = UNIT_START[chain]
    return VECTOR_ROWS + start + step * a


def unit_count(chain):
    return 2 * len(feeds(chain))


def half_of():
    top = lax.axis_size("gy") // 2
    flip = jnp.where(jnp.bitwise_and(lax.axis_index("gy"), top) == 0, 0, 1)
    return jnp.bitwise_xor(lax.axis_index("gx"), flip)


def keep_record(ref, values):
    for chain in range(6):
        for a in (0, 1):
            carries, units = values[chain][a]
            ref[pl.ds(vector_row(chain, a), 8), :] = carries
            count = unit_count(chain)
            ref[pl.ds(unit_row(chain, a), count), :] = units[:count]


def spread(ref, row, count):
    return ref[pl.ds(row, count, stride=0), :]


def call(kernel, name, outs, ins, scratch=(), specs=None, out_specs=None, aliases={}):
    return pl.pallas_call(
        kernel,
        name=name,
        out_shape=[jax.ShapeDtypeStruct(s, jnp.float32) for s in outs],
        in_specs=specs or [VMEM] * len(ins),
        out_specs=out_specs or [VMEM] * len(outs),
        scratch_shapes=list(scratch),
        input_output_aliases=aliases,
        compiler_params=pltpu.CompilerParams(vmem_limit_bytes=8 << 20),
    )(*ins)


def pack_kernel(half, vectors, away, krylov, inverse, back, front, left, right, out, sems):
    core, part = lax.axis_index("gx"), half_of()
    position = 1 - part if away else part
    lanes = pl.ds(pl.multiple_of(position * half, half), half)
    base = (0, vectors, vectors + 2, vectors + 4, vectors + 6)

    def copy(ref, number):
        target = out.at[:, pl.ds(base[number], ref.shape[2])]
        return pltpu.make_async_copy(ref.at[0, :, :, :, lanes], target, sems.at[number])

    plan = [copy(ref, number) for number, ref in enumerate((krylov, inverse, left, right))]
    for one in plan:
        one.start()
    for own, ref in ((0, front), (1, back)):

        @pl.when(core == own)
        def _():
            one = copy(ref, 4)
            one.start()
            one.wait()

    for one in plan:
        one.wait()


def local_kernel(lines, vectors, keep, recv, edge, first, second, low, data, maps):
    core = lax.axis_index("gx")
    pitch = 2 * vectors + 16
    rows = lines * pitch
    width = vectors + 2 * UNITS
    mine, other = keep[...], recv[...]
    data[pl.ds(0, rows), :] = jnp.where(core == 0, mine, other)
    data[pl.ds(rows, rows), :] = jnp.where(core == 0, other, mine)

    def block(plane, number):
        start = plane * rows + 2 * vectors + 4 * number
        return [[data[pl.ds(start + 2 * a + b, lines, stride=pitch), :] for b in (0, 1)] for a in (0, 1)]

    def keep_map(number, left, right):
        for a in (0, 1):
            for b in (0, 1):
                value = -(left[a][0] * right[0][b] + left[a][1] * right[1][b])
                maps[pl.ds((4 * number + 2 * a + b) * lines, lines), :] = value

    for plane in (0, 1):
        inverse = block(plane, 0)
        keep_map(2 * plane, inverse, block(plane, 1))
        keep_map(2 * plane + 1, inverse, block(plane, 2))
        keep_map(4 + plane, inverse, block(plane, 3))

    def product(ref, place, state):
        out = []
        for a in (0, 1):
            left, right = (spread(ref, place(a, b), 8) for b in (0, 1))
            out.append([left * x + right * y for x, y in zip(state[0], state[1])])
        return out

    def mapped(number, line, state):
        return product(maps, lambda a, b: (4 * number + 2 * a + b) * lines + line, state)

    def add(x, y):
        return [[p + q for p, q in zip(s, t)] for s, t in zip(x, y)]

    row = lax.broadcasted_iota(jnp.int32, (8, 128), 0)
    none = jnp.zeros((8, 128), jnp.float32)

    def unit(chain):
        one = [jnp.where(row == 2 * chain + a, 1.0, 0.0) for a in (0, 1)] if chain < UNITS else [none, none]
        return [[none, one[a]] for a in (0, 1)]

    def scaled(plane, line):
        start = plane * rows + line * pitch
        source = [[data[pl.ds(start + a, vectors, stride=2), :]] for a in (0, 1)]
        got = product(data, lambda a, b: start + 2 * vectors + 2 * a + b, source)
        return [[s[0], none] for s in got]

    leaving = [None] * 6

    def solve(plane, chain, source):
        state, states = unit(chain), []
        for line in range(lines):
            state = add(source(line), mapped(2 * plane, line, state))
            states.append(state)
        leaving[chain] = state
        state, result = unit(chain + 1), [None] * lines
        for line in reversed(range(lines)):
            state = add(states[line], mapped(2 * plane + 1, line, state))
            result[line] = state
        leaving[chain + 1] = state
        return result

    swept_low = solve(0, T1, lambda line: scaled(0, line))
    for line in range(lines):
        for a in (0, 1):
            low[pl.ds((2 * line + a) * 8, 8), :] = swept_low[line][a][1]
    swept_high = solve(1, T2, lambda line: add(scaled(1, line), mapped(5, line, swept_low[line])))
    fixed = solve(0, T3, lambda line: mapped(4, line, swept_high[line]))
    keep_record(edge, leaving)
    for line in range(lines):
        total = add(swept_low[line], fixed[line])
        for a in (0, 1):
            for half in (0, 1):
                place = pl.ds((2 * line + a) * width + half * 8, 8)
                first[place, :] = total[a][half]
                second[place, :] = swept_high[line][a][half]


def times(ref, row, step, state):
    out = []
    for a in (0, 1):
        left, right = spread(ref, row + step * a, 8), spread(ref, row + step * a + 1, 8)
        out.append([left * x + right * y for x, y in zip(state[0], state[1])])
    return out


def response(ref, to, frm, state):
    if frm >= UNITS:
        to, frm = to - UNITS, frm - UNITS
    start, step = UNIT_START[to]
    return times(ref, VECTOR_ROWS + start + 2 * frm, step, state)


def total(first, *others):
    for other in others:
        first = [[p + q for p, q in zip(s, t)] for s, t in zip(first, other)]
    return first


def merge_kernel(bit, last, mine, other, edge, mids, lower, upper, *pair):
    is_low = jnp.bitwise_and(lax.axis_index("gy"), bit) == 0
    x, y = mine[...], other[...]
    lower[...] = jnp.where(is_low, x, y)
    upper[...] = jnp.where(is_low, y, x)
    row = lax.broadcasted_iota(jnp.int32, (8, 128), 0)
    up = jnp.bitwise_and(row, 2) == 0

    def base(ref, chain, keep_up):
        wanted = (up if keep_up else ~up) & (row < unit_count(chain))
        out = []
        for a in (0, 1):
            units = ref[pl.ds(unit_row(chain, a), 8), :]
            out.append([ref[pl.ds(vector_row(chain, a), 8), :], jnp.where(wanted, units, 0.0)])
        return out

    low = functools.partial(response, lower)
    high = functools.partial(response, upper)
    m = [None] * 6
    m[T1] = base(lower, T1, True)
    m[U1] = total(base(upper, U1, False), high(U1, T1, m[T1]))
    m[T2] = total(base(lower, T2, True), low(T2, U1, m[U1]))
    m[U2] = total(base(upper, U2, False), high(U2, T1, m[T1]), high(U2, T2, m[T2]))
    m[T3] = total(base(lower, T3, True), low(T3, U1, m[U1]), low(T3, U2, m[U2]))
    m[U3] = total(base(upper, U3, False), high(U3, T1, m[T1]), high(U3, T2, m[T2]), high(U3, T3, m[T3]))
    e = [None] * 6
    for chain in range(6):
        ref, of = (upper, high) if CHAINS[chain][0] == 0 else (lower, low)
        through = [c for c in range(chain + 1) if CHAINS[c][0] == CHAINS[chain][0]]
        e[chain] = total(base(ref, chain, CHAINS[chain][0] == 1), *(of(chain, c, m[c]) for c in through))
    keep_record(mids, m)
    if not last:
        keep_record(edge, e)
        return
    next_low = jnp.bitwise_and(lax.axis_index("gy"), 2 * bit) == 0
    for chain in (T1, T2, T3):
        for a in (0, 1):
            place = pl.ds(vector_row(chain, a), 8)
            edge[place, :] = jnp.where(next_low, e[chain][a][0], e[chain + 1][a][0])
    for ref, table in zip(pair, (UP_ROWS, DOWN_ROWS)):
        ref[...] = jnp.zeros_like(ref)
        for (to, frm), (start, step) in table.items():
            for a in (0, 1):
                ref[pl.ds(start + step * a, 2), :] = e[to][a][1][2 * frm : 2 * frm + 2]
    units = pl.ds(VECTOR_ROWS // 2, LAST_UNITS)
    edge[units, :] = jnp.where(next_low, pair[0][...], pair[1][...])


def write_plane(lines, own, enters, first, second, low, target):
    width = 8 + 2 * UNITS

    def columns(ref, start, chains):
        value = None
        for place, chain in chains:
            for b in (0, 1):
                term = spread(ref, start + 2 * place + b, 8) * enters[chain][b][0]
                value = term if value is None else value + term
        return value

    core = lax.axis_index("gx")
    units = [(c, c) for c in range(UNITS)]
    for plane in (0, 1):

        @pl.when(core == (plane if own else 1 - plane))
        def _():
            source = second if plane else first
            for line in range(lines):
                for a in (0, 1):
                    start = (2 * line + a) * width
                    value = source[pl.ds(start, 8), :] + columns(source, start + 8, units)
                    if plane == 0:
                        value = value + columns(low, (2 * line + a) * 8, [(T1, T3), (U1, U3)])
                    target[pl.ds(line * 16 + a, 8, stride=2), :] = value


def finish_kernel(lines, levels, mine, other, *refs):
    mids, (first, second, low, sent, entry, ups, downs) = refs[: levels - 1], refs[levels - 1 :]
    place = lax.axis_index("gy")
    is_low = jnp.bitwise_and(place, 1 << (levels - 1)) == 0
    x, y = mine[...], other[...]
    ups[...] = jnp.where(is_low, x, y)
    downs[...] = jnp.where(is_low, y, x)

    def base(ref, chain, first_chain):
        skip = vector_row(first_chain, 0)
        return [[ref[pl.ds(vector_row(chain, a) - skip, 8), :]] for a in (0, 1)]

    def up(to, frm, state):
        start, step = UP_ROWS[to, frm]
        return times(ups, VECTOR_ROWS // 2 + start, step, state)

    def down(to, frm, state):
        if frm >= UNITS:
            to, frm = to - UNITS, frm - UNITS
        start, step = DOWN_ROWS[to, frm]
        return times(downs, VECTOR_ROWS // 2 + start, step, state)

    m = [None] * 6
    m[T1] = base(ups, T1, T1)
    m[U1] = total(base(downs, U1, U1), down(U1, T1, m[T1]))
    m[T2] = total(base(ups, T2, T1), up(T2, U1, m[U1]))
    m[U2] = total(base(downs, U2, U1), down(U2, T1, m[T1]), down(U2, T2, m[T2]))
    m[T3] = total(base(ups, T3, T1), up(T3, U1, m[U1]), up(T3, U2, m[U2]))
    m[U3] = total(base(downs, U3, U1), down(U3, T1, m[T1]), down(U3, T2, m[T2]), down(U3, T3, m[T3]))

    def select(condition, x, y):
        return [[jnp.where(condition, p, q) for p, q in zip(s, t)] for s, t in zip(x, y)]

    none = [[jnp.zeros((8, 128), jnp.float32)], [jnp.zeros((8, 128), jnp.float32)]]
    enters = [none] * 6
    for level in reversed(range(levels)):
        if level < levels - 1:
            ref = mids[level]
            m = []
            for chain in range(6):
                terms = [response(ref, chain, c, enters[c]) for c in feeds(chain)]
                if chain >= UNITS:
                    terms += [response(ref, chain, c, enters[c]) for c in range(UNITS, chain + 1)]
                m.append(total(base(ref, chain, T1), *terms))
        is_low = jnp.bitwise_and(place, 1 << level) == 0
        enters = [
            select(is_low, enters[c], m[c]) if CHAINS[c][0] == 0 else select(is_low, m[c], enters[c])
            for c in range(6)
        ]

    write_plane(lines, False, enters, first, second, low, sent)
    for chain in range(6):
        for a in (0, 1):
            entry[pl.ds(vector_row(chain, a), 8), :] = enters[chain][a][0]


def part_copy(half, position, value, out, sem):
    lanes = pl.ds(pl.multiple_of(position * half, half), half)
    return pltpu.make_async_copy(value, out.at[0, :, :, :, lanes], sem)


def own_kernel(lines, entry, first, second, low, kept):
    enters = [[[entry[pl.ds(vector_row(chain, a), 8), :]] for a in (0, 1)] for chain in range(6)]
    write_plane(lines, True, enters, first, second, low, kept)


def store_kernel(half, kept, out, sem):
    one = part_copy(half, half_of(), kept, out, sem.at[0])
    one.start()
    one.wait()


def last_kernel(half, got, before, out, sem):
    one = part_copy(half, 1 - half_of(), got, out, sem.at[0])
    one.start()
    one.wait()


def per_device(krylov, inverse, back, front, left, right):
    _, lines, vectors, _, cells = krylov.shape
    count = lax.axis_size("gy")
    levels = count.bit_length() - 1
    half = cells // 2
    width = vectors + 2 * UNITS
    assert lax.axis_size("gx") == 2 and count == 1 << levels and levels > 1
    assert vectors == 8 and half == 128
    swap = [(0, 1), (1, 0)]

    arguments = [pltpu.with_memory_space_constraint(x, pltpu.HBM) for x in (krylov, inverse, back, front, left, right)]

    def pack(away):
        (out,) = call(
            functools.partial(pack_kernel, half, vectors, away),
            "pack_away" if away else "pack_own",
            [(lines, vectors + 8, 2, half)],
            arguments,
            [pltpu.SemaphoreType.DMA((5,))],
            specs=[HBM] * 6,
        )
        return out.reshape(-1, half)

    recv = lax.ppermute(pack(True), "gx", swap)
    keep = pack(False)
    edge, first, second, low = call(
        functools.partial(local_kernel, lines, vectors),
        "local",
        [(ROWS, half), (2 * lines * width, half), (2 * lines * width, half), (2 * lines * 8, half)],
        (keep, recv),
        [pltpu.VMEM((2 * keep.shape[0], half), jnp.float32), pltpu.VMEM((24 * lines, half), jnp.float32)],
    )
    mids = []
    for level in range(levels - 1):
        got = lax.ppermute(edge, "gy", [(j, j ^ (1 << level)) for j in range(count)])
        last = level == levels - 2
        edge, mid = call(
            functools.partial(merge_kernel, 1 << level, last),
            f"merge{level}",
            [(LAST_ROWS if last else ROWS, half), (ROWS, half)],
            (edge, got),
            [pltpu.VMEM((ROWS, half), jnp.float32)] * 2 + [pltpu.VMEM((LAST_UNITS, half), jnp.float32)] * (2 * last),
        )
        mids.append(mid)
    across = [(core * count + j, (1 - core) * count + (j ^ (count // 2))) for core in (0, 1) for j in range(count)]
    got = lax.ppermute(edge, ("gx", "gy"), across)
    sent, entry = call(
        functools.partial(finish_kernel, lines, levels),
        "finish",
        [(lines * 16, half), (VECTOR_ROWS, half)],
        (edge, got, *mids, first, second, low),
        [pltpu.VMEM((LAST_ROWS, half), jnp.float32)] * 2,
    )
    got = lax.ppermute(sent, "gx", swap)
    (kept,) = call(
        functools.partial(own_kernel, lines), "own", [(lines * 16, half)], (entry, first, second, low)
    )
    (out,) = call(
        functools.partial(store_kernel, half),
        "store",
        [krylov.shape],
        [kept.reshape(lines, vectors, 2, half)],
        [pltpu.SemaphoreType.DMA((1,))],
        specs=[ANY],
        out_specs=[HBM],
    )
    (out,) = call(
        functools.partial(last_kernel, half),
        "last",
        [krylov.shape],
        [got.reshape(lines, vectors, 2, half), out],
        [pltpu.SemaphoreType.DMA((1,))],
        specs=[ANY, HBM],
        out_specs=[HBM],
        aliases={1: 0},
    )
    return out


def solution(mesh):
    spec = P("gx", "gy", None, None, None)
    return jax.shard_map(
        per_device, mesh=mesh, in_specs=(spec,) * 6, out_specs=spec, check_vma=False
    )
```

```python
import functools

import jax
import jax.numpy as jnp
from jax import lax
from jax.experimental import pallas as pl
from jax.experimental.pallas import tpu as pltpu
from jax.sharding import PartitionSpec as P

CHAINS = ((0, 0), (1, 0), (0, 1), (1, 1), (0, 2), (1, 2))
T1, U1, T2, U2, T3, U3 = range(6)
UNITS = 4
VMEM = pl.BlockSpec(memory_space=pltpu.VMEM)
ANY = pl.BlockSpec(memory_space=pl.ANY)
HBM = pl.BlockSpec(memory_space=pltpu.HBM)


def spot(chain):
    direction, number = CHAINS[chain]
    return 3 * direction + number


def feeds(chain):
    return range(min(chain + 1, UNITS))


UNIT_START = {U1: (0, 4), T2: (8, 8), T1: (14, 8), U2: (24, 8), T3: (40, 8), U3: (56, 8)}
VECTOR_ROWS = 96
ROWS = VECTOR_ROWS + 72
UP_ROWS = {(T2, U1): (0, 2), (T3, U1): (4, 4), (T3, U2): (6, 4)}
DOWN_ROWS = {(U1, T1): (0, 2), (U2, T1): (4, 4), (U2, T2): (6, 4), (U3, T1): (12, 4), (U3, T2): (14, 4)}
LAST_UNITS = 24
LAST_ROWS = VECTOR_ROWS // 2 + LAST_UNITS


def vector_row(chain, a):
    return (2 * spot(chain) + a) * 8


def unit_row(chain, a):
    start, step = UNIT_START[chain]
    return VECTOR_ROWS + start + step * a


def unit_count(chain):
    return 2 * len(feeds(chain))


def half_of():
    top = lax.axis_size("gy") // 2
    flip = jnp.where(jnp.bitwise_and(lax.axis_index("gy"), top) == 0, 0, 1)
    return jnp.bitwise_xor(lax.axis_index("gx"), flip)


def keep_record(ref, values, chains=range(6)):
    for chain in chains:
        for a in (0, 1):
            carries, units = values[chain][a]
            ref[pl.ds(vector_row(chain, a), 8), :] = carries
            count = unit_count(chain)
            ref[pl.ds(unit_row(chain, a), count), :] = units[:count]


def spread(ref, row, count):
    return ref[pl.ds(row, count, stride=0), :]


def call(kernel, name, outs, ins, scratch=(), specs=None, out_specs=None, aliases={}):
    return pl.pallas_call(
        kernel,
        name=name,
        out_shape=[jax.ShapeDtypeStruct(s, jnp.float32) for s in outs],
        in_specs=specs or [VMEM] * len(ins),
        out_specs=out_specs or [VMEM] * len(outs),
        scratch_shapes=list(scratch),
        input_output_aliases=aliases,
        compiler_params=pltpu.CompilerParams(vmem_limit_bytes=8 << 20),
    )(*ins)


def pack_kernel(half, vectors, away, krylov, inverse, back, front, left, right, out, sems):
    core, part = lax.axis_index("gx"), half_of()
    position = 1 - part if away else part
    lanes = pl.ds(pl.multiple_of(position * half, half), half)
    base = (0, vectors, vectors + 2, vectors + 4, vectors + 6)

    def copy(ref, number):
        target = out.at[:, pl.ds(base[number], ref.shape[2])]
        return pltpu.make_async_copy(ref.at[0, :, :, :, lanes], target, sems.at[number])

    plan = [copy(ref, number) for number, ref in enumerate((krylov, inverse, left, right))]
    for one in plan:
        one.start()
    for own, ref in ((0, front), (1, back)):

        @pl.when(core == own)
        def _():
            one = copy(ref, 4)
            one.start()
            one.wait()

    for one in plan:
        one.wait()


def combine(ref, place, state):
    out = []
    for a in (0, 1):
        left, right = (spread(ref, place(a, b), 8) for b in (0, 1))
        out.append([left * x + right * y for x, y in zip(state[0], state[1])])
    return out


def add(x, y):
    return [[p + q for p, q in zip(s, t)] for s, t in zip(x, y)]


FORWARD, BACKWARD, ACROSS = range(3)


def make_maps(lines, vectors, data, maps):
    pitch = 2 * vectors + 16

    def block(number):
        start = 2 * vectors + 4 * number
        return [[data[pl.ds(start + 2 * a + b, lines, stride=pitch), :] for b in (0, 1)] for a in (0, 1)]

    inverse = block(0)
    for number in (FORWARD, BACKWARD, ACROSS):
        coupling = block(1 + number)
        for a in (0, 1):
            for b in (0, 1):
                value = -(inverse[a][0] * coupling[0][b] + inverse[a][1] * coupling[1][b])
                maps[pl.ds((4 * number + 2 * a + b) * lines, lines), :] = value


def mapped(lines, maps, number, line, state):
    return combine(maps, lambda a, b: (4 * number + 2 * a + b) * lines + line, state)


def scaled(vectors, data, line):
    start = line * (2 * vectors + 16)
    source = [[data[pl.ds(start + a, vectors, stride=2), :]] for a in (0, 1)]
    got = combine(data, lambda a, b: start + 2 * vectors + 2 * a + b, source)
    return [[s[0], jnp.zeros((8, 128), jnp.float32)] for s in got]


def unit(chain):
    row = lax.broadcasted_iota(jnp.int32, (8, 128), 0)
    none = jnp.zeros((8, 128), jnp.float32)
    one = [jnp.where(row == 2 * chain + a, 1.0, 0.0) if chain < UNITS else none for a in (0, 1)]
    return [[none, one[a]] for a in (0, 1)]


def sweep_plane(lines, maps, chain, source, leaving):
    state, states = unit(chain), []
    for line in range(lines):
        state = add(source(line), mapped(lines, maps, FORWARD, line, state))
        states.append(state)
    leaving[chain] = state
    state, result = unit(chain + 1), [None] * lines
    for line in reversed(range(lines)):
        state = add(states[line], mapped(lines, maps, BACKWARD, line, state))
        result[line] = state
    leaving[chain + 1] = state
    return result


def state_rows(line, a, part):
    return pl.ds((2 * line + a) * (8 + 2 * UNITS) + 8 * part, 8)


def early_kernel(lines, vectors, keep, swept, edge, maps):
    make_maps(lines, vectors, keep, maps)

    @pl.when(lax.axis_index("gx") == 0)
    def _():
        leaving = [None] * 6
        result = sweep_plane(lines, maps, T1, lambda line: scaled(vectors, keep, line), leaving)
        keep_record(edge, leaving, (T1, U1))
        for line in range(lines):
            for a in (0, 1):
                for part in (0, 1):
                    swept[state_rows(line, a, part), :] = result[line][a][part]


def local_kernel(lines, vectors, keep, recv, swept, early, own_maps, edge, first, second, low, other_maps):
    make_maps(lines, vectors, recv, other_maps)
    for own in (0, 1):

        @pl.when(lax.axis_index("gx") == own)
        def _():
            leaving = [None] * 6
            maps = (other_maps, own_maps) if own else (own_maps, other_maps)
            if own == 0:
                swept_low = [
                    [[swept[state_rows(line, a, part), :] for part in (0, 1)] for a in (0, 1)] for line in range(lines)
                ]
                for chain in (T1, U1):
                    leaving[chain] = [
                        [early[pl.ds(vector_row(chain, a), 8), :], early[pl.ds(unit_row(chain, a), 8), :]] for a in (0, 1)
                    ]
            else:
                swept_low = sweep_plane(lines, maps[0], T1, lambda line: scaled(vectors, recv, line), leaving)
            high_data = keep if own else recv
            swept_high = sweep_plane(
                lines,
                maps[1],
                T2,
                lambda line: add(scaled(vectors, high_data, line), mapped(lines, maps[1], ACROSS, line, swept_low[line])),
                leaving,
            )
            fixed = sweep_plane(
                lines, maps[0], T3, lambda line: mapped(lines, maps[0], ACROSS, line, swept_high[line]), leaving
            )
            keep_record(edge, leaving)
            for line in range(lines):
                total = add(swept_low[line], fixed[line])
                for a in (0, 1):
                    low[pl.ds((2 * line + a) * 8, 8), :] = swept_low[line][a][1]
                    for part in (0, 1):
                        first[state_rows(line, a, part), :] = total[a][part]
                        second[state_rows(line, a, part), :] = swept_high[line][a][part]


def times(ref, row, step, state):
    out = []
    for a in (0, 1):
        left, right = spread(ref, row + step * a, 8), spread(ref, row + step * a + 1, 8)
        out.append([left * x + right * y for x, y in zip(state[0], state[1])])
    return out


def response(ref, to, frm, state):
    if frm >= UNITS:
        to, frm = to - UNITS, frm - UNITS
    start, step = UNIT_START[to]
    return times(ref, VECTOR_ROWS + start + 2 * frm, step, state)


def total(first, *others):
    for other in others:
        first = [[p + q for p, q in zip(s, t)] for s, t in zip(first, other)]
    return first


def merge_kernel(bit, last, mine, other, edge, mids, lower, upper, *pair):
    is_low = jnp.bitwise_and(lax.axis_index("gy"), bit) == 0
    x, y = mine[...], other[...]
    lower[...] = jnp.where(is_low, x, y)
    upper[...] = jnp.where(is_low, y, x)
    row = lax.broadcasted_iota(jnp.int32, (8, 128), 0)
    up = jnp.bitwise_and(row, 2) == 0

    def base(ref, chain, keep_up):
        wanted = (up if keep_up else ~up) & (row < unit_count(chain))
        out = []
        for a in (0, 1):
            units = ref[pl.ds(unit_row(chain, a), 8), :]
            out.append([ref[pl.ds(vector_row(chain, a), 8), :], jnp.where(wanted, units, 0.0)])
        return out

    low = functools.partial(response, lower)
    high = functools.partial(response, upper)
    m = [None] * 6
    m[T1] = base(lower, T1, True)
    m[U1] = total(base(upper, U1, False), high(U1, T1, m[T1]))
    m[T2] = total(base(lower, T2, True), low(T2, U1, m[U1]))
    m[U2] = total(base(upper, U2, False), high(U2, T1, m[T1]), high(U2, T2, m[T2]))
    m[T3] = total(base(lower, T3, True), low(T3, U1, m[U1]), low(T3, U2, m[U2]))
    m[U3] = total(base(upper, U3, False), high(U3, T1, m[T1]), high(U3, T2, m[T2]), high(U3, T3, m[T3]))
    e = [None] * 6
    for chain in range(6):
        ref, of = (upper, high) if CHAINS[chain][0] == 0 else (lower, low)
        through = [c for c in range(chain + 1) if CHAINS[c][0] == CHAINS[chain][0]]
        e[chain] = total(base(ref, chain, CHAINS[chain][0] == 1), *(of(chain, c, m[c]) for c in through))
    keep_record(mids, m)
    if not last:
        keep_record(edge, e)
        return
    next_low = jnp.bitwise_and(lax.axis_index("gy"), 2 * bit) == 0
    for chain in (T1, T2, T3):
        for a in (0, 1):
            place = pl.ds(vector_row(chain, a), 8)
            edge[place, :] = jnp.where(next_low, e[chain][a][0], e[chain + 1][a][0])
    for ref, table in zip(pair, (UP_ROWS, DOWN_ROWS)):
        ref[...] = jnp.zeros_like(ref)
        for (to, frm), (start, step) in table.items():
            for a in (0, 1):
                ref[pl.ds(start + step * a, 2), :] = e[to][a][1][2 * frm : 2 * frm + 2]
    units = pl.ds(VECTOR_ROWS // 2, LAST_UNITS)
    edge[units, :] = jnp.where(next_low, pair[0][...], pair[1][...])


def write_plane(lines, own, enters, first, second, low, target):
    width = 8 + 2 * UNITS

    def columns(ref, start, chains):
        value = None
        for place, chain in chains:
            for b in (0, 1):
                term = spread(ref, start + 2 * place + b, 8) * enters[chain][b][0]
                value = term if value is None else value + term
        return value

    core = lax.axis_index("gx")
    units = [(c, c) for c in range(UNITS)]
    for plane in (0, 1):

        @pl.when(core == (plane if own else 1 - plane))
        def _():
            source = second if plane else first
            for line in range(lines):
                for a in (0, 1):
                    start = (2 * line + a) * width
                    value = source[pl.ds(start, 8), :] + columns(source, start + 8, units)
                    if plane == 0:
                        value = value + columns(low, (2 * line + a) * 8, [(T1, T3), (U1, U3)])
                    target[pl.ds(line * 16 + a, 8, stride=2), :] = value


def finish_kernel(lines, levels, mine, other, *refs):
    mids, (first, second, low, sent, entry, ups, downs) = refs[: levels - 1], refs[levels - 1 :]
    place = lax.axis_index("gy")
    is_low = jnp.bitwise_and(place, 1 << (levels - 1)) == 0
    x, y = mine[...], other[...]
    ups[...] = jnp.where(is_low, x, y)
    downs[...] = jnp.where(is_low, y, x)

    def base(ref, chain, first_chain):
        skip = vector_row(first_chain, 0)
        return [[ref[pl.ds(vector_row(chain, a) - skip, 8), :]] for a in (0, 1)]

    def up(to, frm, state):
        start, step = UP_ROWS[to, frm]
        return times(ups, VECTOR_ROWS // 2 + start, step, state)

    def down(to, frm, state):
        if frm >= UNITS:
            to, frm = to - UNITS, frm - UNITS
        start, step = DOWN_ROWS[to, frm]
        return times(downs, VECTOR_ROWS // 2 + start, step, state)

    m = [None] * 6
    m[T1] = base(ups, T1, T1)
    m[U1] = total(base(downs, U1, U1), down(U1, T1, m[T1]))
    m[T2] = total(base(ups, T2, T1), up(T2, U1, m[U1]))
    m[U2] = total(base(downs, U2, U1), down(U2, T1, m[T1]), down(U2, T2, m[T2]))
    m[T3] = total(base(ups, T3, T1), up(T3, U1, m[U1]), up(T3, U2, m[U2]))
    m[U3] = total(base(downs, U3, U1), down(U3, T1, m[T1]), down(U3, T2, m[T2]), down(U3, T3, m[T3]))

    def select(condition, x, y):
        return [[jnp.where(condition, p, q) for p, q in zip(s, t)] for s, t in zip(x, y)]

    none = [[jnp.zeros((8, 128), jnp.float32)], [jnp.zeros((8, 128), jnp.float32)]]
    enters = [none] * 6
    for level in reversed(range(levels)):
        if level < levels - 1:
            ref = mids[level]
            m = []
            for chain in range(6):
                terms = [response(ref, chain, c, enters[c]) for c in feeds(chain)]
                if chain >= UNITS:
                    terms += [response(ref, chain, c, enters[c]) for c in range(UNITS, chain + 1)]
                m.append(total(base(ref, chain, T1), *terms))
        is_low = jnp.bitwise_and(place, 1 << level) == 0
        enters = [
            select(is_low, enters[c], m[c]) if CHAINS[c][0] == 0 else select(is_low, m[c], enters[c])
            for c in range(6)
        ]

    write_plane(lines, False, enters, first, second, low, sent)
    for chain in range(6):
        for a in (0, 1):
            entry[pl.ds(vector_row(chain, a), 8), :] = enters[chain][a][0]


def part_copy(half, position, value, out, sem):
    lanes = pl.ds(pl.multiple_of(position * half, half), half)
    return pltpu.make_async_copy(value, out.at[0, :, :, :, lanes], sem)


def own_kernel(lines, entry, first, second, low, kept):
    enters = [[[entry[pl.ds(vector_row(chain, a), 8), :]] for a in (0, 1)] for chain in range(6)]
    write_plane(lines, True, enters, first, second, low, kept)


def store_kernel(half, kept, out, sem):
    one = part_copy(half, half_of(), kept, out, sem.at[0])
    one.start()
    one.wait()


def last_kernel(half, got, before, out, sem):
    one = part_copy(half, 1 - half_of(), got, out, sem.at[0])
    one.start()
    one.wait()


def per_device(krylov, inverse, back, front, left, right):
    _, lines, vectors, _, cells = krylov.shape
    count = lax.axis_size("gy")
    levels = count.bit_length() - 1
    half = cells // 2
    width = vectors + 2 * UNITS
    assert lax.axis_size("gx") == 2 and count == 1 << levels and levels > 1
    assert vectors == 8 and half == 128
    swap = [(0, 1), (1, 0)]

    arguments = [pltpu.with_memory_space_constraint(x, pltpu.HBM) for x in (krylov, inverse, back, front, left, right)]

    def pack(away):
        (out,) = call(
            functools.partial(pack_kernel, half, vectors, away),
            "pack_away" if away else "pack_own",
            [(lines, vectors + 8, 2, half)],
            arguments,
            [pltpu.SemaphoreType.DMA((5,))],
            specs=[HBM] * 6,
        )
        return out.reshape(-1, half)

    recv = lax.ppermute(pack(True), "gx", swap)
    keep = pack(False)
    swept, early, own_maps = call(
        functools.partial(early_kernel, lines, vectors),
        "early",
        [(2 * lines * width, half), (ROWS, half), (12 * lines, half)],
        (keep,),
    )
    edge, first, second, low = call(
        functools.partial(local_kernel, lines, vectors),
        "local",
        [(ROWS, half), (2 * lines * width, half), (2 * lines * width, half), (2 * lines * 8, half)],
        (keep, recv, swept, early, own_maps),
        [pltpu.VMEM((12 * lines, half), jnp.float32)],
    )
    mids = []
    for level in range(levels - 1):
        got = lax.ppermute(edge, "gy", [(j, j ^ (1 << level)) for j in range(count)])
        last = level == levels - 2
        edge, mid = call(
            functools.partial(merge_kernel, 1 << level, last),
            f"merge{level}",
            [(LAST_ROWS if last else ROWS, half), (ROWS, half)],
            (edge, got),
            [pltpu.VMEM((ROWS, half), jnp.float32)] * 2 + [pltpu.VMEM((LAST_UNITS, half), jnp.float32)] * (2 * last),
        )
        mids.append(mid)
    across = [(core * count + j, (1 - core) * count + (j ^ (count // 2))) for core in (0, 1) for j in range(count)]
    got = lax.ppermute(edge, ("gx", "gy"), across)
    sent, entry = call(
        functools.partial(finish_kernel, lines, levels),
        "finish",
        [(lines * 16, half), (VECTOR_ROWS, half)],
        (edge, got, *mids, first, second, low),
        [pltpu.VMEM((LAST_ROWS, half), jnp.float32)] * 2,
    )
    got = lax.ppermute(sent, "gx", swap)
    (kept,) = call(
        functools.partial(own_kernel, lines), "own", [(lines * 16, half)], (entry, first, second, low)
    )
    (out,) = call(
        functools.partial(store_kernel, half),
        "store",
        [krylov.shape],
        [kept.reshape(lines, vectors, 2, half)],
        [pltpu.SemaphoreType.DMA((1,))],
        specs=[ANY],
        out_specs=[HBM],
    )
    (out,) = call(
        functools.partial(last_kernel, half),
        "last",
        [krylov.shape],
        [got.reshape(lines, vectors, 2, half), out],
        [pltpu.SemaphoreType.DMA((1,))],
        specs=[ANY, HBM],
        out_specs=[HBM],
        aliases={1: 0},
    )
    return out


def solution(mesh):
    spec = P("gx", "gy", None, None, None)
    return jax.shard_map(
        per_device, mesh=mesh, in_specs=(spec,) * 6, out_specs=spec, check_vma=False
    )
```

```python
import functools

import jax
import jax.numpy as jnp
from jax import lax
from jax.experimental import pallas as pl
from jax.experimental.pallas import tpu as pltpu
from jax.sharding import PartitionSpec as P

CHAINS = ((0, 0), (1, 0), (0, 1), (1, 1), (0, 2), (1, 2))
T1, U1, T2, U2, T3, U3 = range(6)
UNITS = 4
VMEM = pl.BlockSpec(memory_space=pltpu.VMEM)
ANY = pl.BlockSpec(memory_space=pl.ANY)
HBM = pl.BlockSpec(memory_space=pltpu.HBM)


def spot(chain):
    direction, number = CHAINS[chain]
    return 3 * direction + number


def feeds(chain):
    return range(min(chain + 1, UNITS))


UNIT_START = {U1: (0, 4), T2: (8, 8), T1: (14, 8), U2: (24, 8), T3: (40, 8), U3: (56, 8)}
VECTOR_ROWS = 96
ROWS = VECTOR_ROWS + 72
UP_ROWS = {(T2, U1): (0, 2), (T3, U1): (4, 4), (T3, U2): (6, 4)}
DOWN_ROWS = {(U1, T1): (0, 2), (U2, T1): (4, 4), (U2, T2): (6, 4), (U3, T1): (12, 4), (U3, T2): (14, 4)}
LAST_UNITS = 24
LAST_ROWS = VECTOR_ROWS // 2 + LAST_UNITS


def vector_row(chain, a):
    return (2 * spot(chain) + a) * 8


def unit_row(chain, a):
    start, step = UNIT_START[chain]
    return VECTOR_ROWS + start + step * a


def unit_count(chain):
    return 2 * len(feeds(chain))


def half_of():
    top = lax.axis_size("gy") // 2
    flip = jnp.where(jnp.bitwise_and(lax.axis_index("gy"), top) == 0, 0, 1)
    return jnp.bitwise_xor(lax.axis_index("gx"), flip)


def keep_record(ref, values, chains=range(6)):
    for chain in chains:
        for a in (0, 1):
            carries, units = values[chain][a]
            ref[pl.ds(vector_row(chain, a), 8), :] = carries
            count = unit_count(chain)
            ref[pl.ds(unit_row(chain, a), count), :] = units[:count]


def spread(ref, row, count):
    return ref[pl.ds(row, count, stride=0), :]


def call(kernel, name, outs, ins, scratch=(), specs=None, out_specs=None, aliases={}):
    return pl.pallas_call(
        kernel,
        name=name,
        out_shape=[jax.ShapeDtypeStruct(s, jnp.float32) for s in outs],
        in_specs=specs or [VMEM] * len(ins),
        out_specs=out_specs or [VMEM] * len(outs),
        scratch_shapes=list(scratch),
        input_output_aliases=aliases,
        compiler_params=pltpu.CompilerParams(vmem_limit_bytes=8 << 20),
    )(*ins)


def pack_kernel(half, vectors, away, krylov, inverse, back, front, left, right, out, sems):
    core, part = lax.axis_index("gx"), half_of()
    position = 1 - part if away else part
    lanes = pl.ds(pl.multiple_of(position * half, half), half)
    base = (0, vectors, vectors + 2, vectors + 4, vectors + 6)

    def copy(ref, number):
        target = out.at[:, pl.ds(base[number], ref.shape[2])]
        return pltpu.make_async_copy(ref.at[0, :, :, :, lanes], target, sems.at[number])

    plan = [copy(ref, number) for number, ref in enumerate((krylov, inverse, left, right))]
    for one in plan:
        one.start()
    for own, ref in ((0, front), (1, back)):

        @pl.when(core == own)
        def _():
            one = copy(ref, 4)
            one.start()
            one.wait()

    for one in plan:
        one.wait()


def combine(ref, place, state):
    out = []
    for a in (0, 1):
        left, right = (spread(ref, place(a, b), 8) for b in (0, 1))
        out.append([left * x + right * y for x, y in zip(state[0], state[1])])
    return out


def add(x, y):
    return [[p + q for p, q in zip(s, t)] for s, t in zip(x, y)]


FORWARD, BACKWARD, ACROSS = range(3)


def make_maps(lines, vectors, data, maps):
    pitch = 2 * vectors + 16

    def block(number):
        start = 2 * vectors + 4 * number
        return [[data[pl.ds(start + 2 * a + b, lines, stride=pitch), :] for b in (0, 1)] for a in (0, 1)]

    inverse = block(0)
    for number in (FORWARD, BACKWARD, ACROSS):
        coupling = block(1 + number)
        for a in (0, 1):
            for b in (0, 1):
                value = -(inverse[a][0] * coupling[0][b] + inverse[a][1] * coupling[1][b])
                maps[pl.ds((4 * number + 2 * a + b) * lines, lines), :] = value


def mapped(lines, maps, number, line, state):
    return combine(maps, lambda a, b: (4 * number + 2 * a + b) * lines + line, state)


def scaled(vectors, data, line):
    start = line * (2 * vectors + 16)
    source = [[data[pl.ds(start + a, vectors, stride=2), :]] for a in (0, 1)]
    got = combine(data, lambda a, b: start + 2 * vectors + 2 * a + b, source)
    return [[s[0], jnp.zeros((8, 128), jnp.float32)] for s in got]


def unit(chain):
    row = lax.broadcasted_iota(jnp.int32, (8, 128), 0)
    none = jnp.zeros((8, 128), jnp.float32)
    one = [jnp.where(row == 2 * chain + a, 1.0, 0.0) if chain < UNITS else none for a in (0, 1)]
    return [[none, one[a]] for a in (0, 1)]


def sweep_plane(lines, maps, chain, source, leaving):
    state, states = unit(chain), []
    for line in range(lines):
        state = add(source(line), mapped(lines, maps, FORWARD, line, state))
        states.append(state)
    leaving[chain] = state
    state, result = unit(chain + 1), [None] * lines
    for line in reversed(range(lines)):
        state = add(states[line], mapped(lines, maps, BACKWARD, line, state))
        result[line] = state
    leaving[chain + 1] = state
    return result


def state_rows(line, a, part):
    return pl.ds((2 * line + a) * (8 + 2 * UNITS) + 8 * part, 8)


def early_kernel(lines, vectors, keep, swept, edge, maps):
    make_maps(lines, vectors, keep, maps)

    @pl.when(lax.axis_index("gx") == 0)
    def _():
        leaving = [None] * 6
        result = sweep_plane(lines, maps, T1, lambda line: scaled(vectors, keep, line), leaving)
        keep_record(edge, leaving, (T1, U1))
        for line in range(lines):
            for a in (0, 1):
                for part in (0, 1):
                    swept[state_rows(line, a, part), :] = result[line][a][part]


def local_kernel(lines, vectors, keep, recv, swept, early, own_maps, edge, first, second, low, other_maps):
    make_maps(lines, vectors, recv, other_maps)
    for own in (0, 1):

        @pl.when(lax.axis_index("gx") == own)
        def _():
            leaving = [None] * 6
            maps = (other_maps, own_maps) if own else (own_maps, other_maps)
            if own == 0:
                swept_low = [
                    [[swept[state_rows(line, a, part), :] for part in (0, 1)] for a in (0, 1)] for line in range(lines)
                ]
                for chain in (T1, U1):
                    leaving[chain] = [
                        [early[pl.ds(vector_row(chain, a), 8), :], early[pl.ds(unit_row(chain, a), 8), :]] for a in (0, 1)
                    ]
            else:
                swept_low = sweep_plane(lines, maps[0], T1, lambda line: scaled(vectors, recv, line), leaving)
            high_data = keep if own else recv
            swept_high = sweep_plane(
                lines,
                maps[1],
                T2,
                lambda line: add(scaled(vectors, high_data, line), mapped(lines, maps[1], ACROSS, line, swept_low[line])),
                leaving,
            )
            fixed = sweep_plane(
                lines, maps[0], T3, lambda line: mapped(lines, maps[0], ACROSS, line, swept_high[line]), leaving
            )
            keep_record(edge, leaving)
            for line in range(lines):
                total = add(swept_low[line], fixed[line])
                for a in (0, 1):
                    low[pl.ds((2 * line + a) * 8, 8), :] = swept_low[line][a][1]
                    for part in (0, 1):
                        first[state_rows(line, a, part), :] = total[a][part]
                        second[state_rows(line, a, part), :] = swept_high[line][a][part]


def times(ref, row, step, state):
    out = []
    for a in (0, 1):
        left, right = spread(ref, row + step * a, 8), spread(ref, row + step * a + 1, 8)
        out.append([left * x + right * y for x, y in zip(state[0], state[1])])
    return out


def response(ref, to, frm, state):
    if frm >= UNITS:
        to, frm = to - UNITS, frm - UNITS
    start, step = UNIT_START[to]
    return times(ref, VECTOR_ROWS + start + 2 * frm, step, state)


def total(first, *others):
    for other in others:
        first = [[p + q for p, q in zip(s, t)] for s, t in zip(first, other)]
    return first


def merge_kernel(bit, last, mine, other, edge, mids, lower, upper, *pair):
    is_low = jnp.bitwise_and(lax.axis_index("gy"), bit) == 0
    x, y = mine[...], other[...]
    lower[...] = jnp.where(is_low, x, y)
    upper[...] = jnp.where(is_low, y, x)
    row = lax.broadcasted_iota(jnp.int32, (8, 128), 0)
    up = jnp.bitwise_and(row, 2) == 0

    def base(ref, chain, keep_up):
        wanted = (up if keep_up else ~up) & (row < unit_count(chain))
        out = []
        for a in (0, 1):
            units = ref[pl.ds(unit_row(chain, a), 8), :]
            out.append([ref[pl.ds(vector_row(chain, a), 8), :], jnp.where(wanted, units, 0.0)])
        return out

    low = functools.partial(response, lower)
    high = functools.partial(response, upper)
    m = [None] * 6
    m[T1] = base(lower, T1, True)
    m[U1] = total(base(upper, U1, False), high(U1, T1, m[T1]))
    m[T2] = total(base(lower, T2, True), low(T2, U1, m[U1]))
    m[U2] = total(base(upper, U2, False), high(U2, T1, m[T1]), high(U2, T2, m[T2]))
    m[T3] = total(base(lower, T3, True), low(T3, U1, m[U1]), low(T3, U2, m[U2]))
    m[U3] = total(base(upper, U3, False), high(U3, T1, m[T1]), high(U3, T2, m[T2]), high(U3, T3, m[T3]))
    e = [None] * 6
    for chain in range(6):
        ref, of = (upper, high) if CHAINS[chain][0] == 0 else (lower, low)
        through = [c for c in range(chain + 1) if CHAINS[c][0] == CHAINS[chain][0]]
        e[chain] = total(base(ref, chain, CHAINS[chain][0] == 1), *(of(chain, c, m[c]) for c in through))
    keep_record(mids, m)
    if not last:
        keep_record(edge, e)
        return
    next_low = jnp.bitwise_and(lax.axis_index("gy"), 2 * bit) == 0
    for chain in (T1, T2, T3):
        for a in (0, 1):
            place = pl.ds(vector_row(chain, a), 8)
            edge[place, :] = jnp.where(next_low, e[chain][a][0], e[chain + 1][a][0])
    for ref, table in zip(pair, (UP_ROWS, DOWN_ROWS)):
        ref[...] = jnp.zeros_like(ref)
        for (to, frm), (start, step) in table.items():
            for a in (0, 1):
                ref[pl.ds(start + step * a, 2), :] = e[to][a][1][2 * frm : 2 * frm + 2]
    units = pl.ds(VECTOR_ROWS // 2, LAST_UNITS)
    edge[units, :] = jnp.where(next_low, pair[0][...], pair[1][...])


def compose_kernel(lines, levels, *refs):
    mids, (first, second, low, own, away) = refs[: levels - 1], refs[levels - 1 :]
    place, core = lax.axis_index("gy"), lax.axis_index("gx")
    row = lax.broadcasted_iota(jnp.int32, (8, 128), 0)
    none = jnp.zeros((8, 128), jnp.float32)
    in_low = jnp.bitwise_and(place, 1 << (levels - 1)) == 0

    def select(condition, x, y):
        return [[jnp.where(condition, p, q) for p, q in zip(s, t)] for s, t in zip(x, y)]

    enters = []
    for direction, number in CHAINS:
        one = [jnp.where(row == 2 * number + a, 1.0, 0.0) for a in (0, 1)]
        here = in_low if direction else ~in_low
        enters.append([[none, jnp.where(here, one[a], 0.0)] for a in (0, 1)])
    for level in reversed(range(levels - 1)):
        ref = mids[level]
        m = []
        for chain in range(6):
            base = [[ref[pl.ds(vector_row(chain, a), 8), :], none] for a in (0, 1)]
            terms = [response(ref, chain, c, enters[c]) for c in feeds(chain)]
            if chain >= UNITS:
                terms += [response(ref, chain, c, enters[c]) for c in range(UNITS, chain + 1)]
            m.append(total(base, *terms))
        is_low = jnp.bitwise_and(place, 1 << level) == 0
        enters = [
            select(is_low, enters[c], m[c]) if CHAINS[c][0] == 0 else select(is_low, m[c], enters[c])
            for c in range(6)
        ]

    width = 8 + 2 * UNITS
    units = [(c, c) for c in range(UNITS)]
    for line in range(lines):
        for a in (0, 1):
            start = (2 * line + a) * width
            planes = []
            for source, extra in ((first, [(T1, T3), (U1, U3)]), (second, [])):
                value = [source[pl.ds(start, 8), :], none]
                pairs = [(source, start + 8, pair) for pair in units]
                pairs += [(low, (2 * line + a) * 8, pair) for pair in extra]
                for ref, begin, (column, chain) in pairs:
                    for b in (0, 1):
                        factor = spread(ref, begin + 2 * column + b, 8)
                        value = [v + factor * e for v, e in zip(value, enters[chain][b])]
                planes.append(value)
            for part in (0, 1):
                mine, other = planes[0][part], planes[1][part]
                own[state_rows(line, a, part), :] = jnp.where(core == 0, mine, other)
                away[state_rows(line, a, part), :] = jnp.where(core == 0, other, mine)


def apply_map(lines, ref, entry, target):
    width = 8 + 2 * UNITS
    for line in range(lines):
        for a in (0, 1):
            start = (2 * line + a) * width
            value = ref[pl.ds(start, 8), :]
            for number in range(3):
                for b in (0, 1):
                    value = value + spread(ref, start + 8 + 2 * number + b, 8) * entry[number][b]
            target[pl.ds(line * 16 + a, 8, stride=2), :] = value


def finish_kernel(lines, levels, mine, other, away, sent, entry, ups, downs):
    is_low = jnp.bitwise_and(lax.axis_index("gy"), 1 << (levels - 1)) == 0
    x, y = mine[...], other[...]
    ups[...] = jnp.where(is_low, x, y)
    downs[...] = jnp.where(is_low, y, x)

    def base(ref, chain, first_chain):
        skip = vector_row(first_chain, 0)
        return [[ref[pl.ds(vector_row(chain, a) - skip, 8), :]] for a in (0, 1)]

    def up(to, frm, state):
        start, step = UP_ROWS[to, frm]
        return times(ups, VECTOR_ROWS // 2 + start, step, state)

    def down(to, frm, state):
        if frm >= UNITS:
            to, frm = to - UNITS, frm - UNITS
        start, step = DOWN_ROWS[to, frm]
        return times(downs, VECTOR_ROWS // 2 + start, step, state)

    m = [None] * 6
    m[T1] = base(ups, T1, T1)
    m[U1] = total(base(downs, U1, U1), down(U1, T1, m[T1]))
    m[T2] = total(base(ups, T2, T1), up(T2, U1, m[U1]))
    m[U2] = total(base(downs, U2, U1), down(U2, T1, m[T1]), down(U2, T2, m[T2]))
    m[T3] = total(base(ups, T3, T1), up(T3, U1, m[U1]), up(T3, U2, m[U2]))
    m[U3] = total(base(downs, U3, U1), down(U3, T1, m[T1]), down(U3, T2, m[T2]), down(U3, T3, m[T3]))
    enters = [
        [jnp.where(is_low, m[2 * number + 1][b][0], m[2 * number][b][0]) for b in (0, 1)] for number in range(3)
    ]
    apply_map(lines, away, enters, sent)
    for number in range(3):
        for b in (0, 1):
            entry[pl.ds((2 * number + b) * 8, 8), :] = enters[number][b]


def own_kernel(lines, entry, own, kept):
    enters = [[entry[pl.ds((2 * number + b) * 8, 8), :] for b in (0, 1)] for number in range(3)]
    apply_map(lines, own, enters, kept)


def part_copy(half, position, value, out, sem):
    lanes = pl.ds(pl.multiple_of(position * half, half), half)
    return pltpu.make_async_copy(value, out.at[0, :, :, :, lanes], sem)


def store_kernel(half, kept, out, sem):
    one = part_copy(half, half_of(), kept, out, sem.at[0])
    one.start()
    one.wait()


def last_kernel(half, got, before, out, sem):
    one = part_copy(half, 1 - half_of(), got, out, sem.at[0])
    one.start()
    one.wait()


def per_device(krylov, inverse, back, front, left, right):
    _, lines, vectors, _, cells = krylov.shape
    count = lax.axis_size("gy")
    levels = count.bit_length() - 1
    half = cells // 2
    width = vectors + 2 * UNITS
    assert lax.axis_size("gx") == 2 and count == 1 << levels and levels > 1
    assert vectors == 8 and half == 128
    swap = [(0, 1), (1, 0)]

    arguments = [pltpu.with_memory_space_constraint(x, pltpu.HBM) for x in (krylov, inverse, back, front, left, right)]

    def pack(away):
        (out,) = call(
            functools.partial(pack_kernel, half, vectors, away),
            "pack_away" if away else "pack_own",
            [(lines, vectors + 8, 2, half)],
            arguments,
            [pltpu.SemaphoreType.DMA((5,))],
            specs=[HBM] * 6,
        )
        return out.reshape(-1, half)

    recv = lax.ppermute(pack(True), "gx", swap)
    keep = pack(False)
    swept, early, own_maps = call(
        functools.partial(early_kernel, lines, vectors),
        "early",
        [(2 * lines * width, half), (ROWS, half), (12 * lines, half)],
        (keep,),
    )
    edge, first, second, low = call(
        functools.partial(local_kernel, lines, vectors),
        "local",
        [(ROWS, half), (2 * lines * width, half), (2 * lines * width, half), (2 * lines * 8, half)],
        (keep, recv, swept, early, own_maps),
        [pltpu.VMEM((12 * lines, half), jnp.float32)],
    )
    mids = []
    for level in range(levels - 1):
        got = lax.ppermute(edge, "gy", [(j, j ^ (1 << level)) for j in range(count)])
        last = level == levels - 2
        edge, mid = call(
            functools.partial(merge_kernel, 1 << level, last),
            f"merge{level}",
            [(LAST_ROWS if last else ROWS, half), (ROWS, half)],
            (edge, got),
            [pltpu.VMEM((ROWS, half), jnp.float32)] * 2 + [pltpu.VMEM((LAST_UNITS, half), jnp.float32)] * (2 * last),
        )
        mids.append(mid)
    across = [(core * count + j, (1 - core) * count + (j ^ (count // 2))) for core in (0, 1) for j in range(count)]
    got = lax.ppermute(edge, ("gx", "gy"), across)
    own, away = call(
        functools.partial(compose_kernel, lines, levels),
        "compose",
        [(2 * lines * width, half)] * 2,
        (*mids, first, second, low),
    )
    sent, entry = call(
        functools.partial(finish_kernel, lines, levels),
        "finish",
        [(lines * 16, half), (VECTOR_ROWS // 2, half)],
        (edge, got, away),
        [pltpu.VMEM((LAST_ROWS, half), jnp.float32)] * 2,
    )
    got = lax.ppermute(sent, "gx", swap)
    (kept,) = call(functools.partial(own_kernel, lines), "own", [(lines * 16, half)], (entry, own))
    (out,) = call(
        functools.partial(store_kernel, half),
        "store",
        [krylov.shape],
        [kept.reshape(lines, vectors, 2, half)],
        [pltpu.SemaphoreType.DMA((1,))],
        specs=[ANY],
        out_specs=[HBM],
    )
    (out,) = call(
        functools.partial(last_kernel, half),
        "last",
        [krylov.shape],
        [got.reshape(lines, vectors, 2, half), out],
        [pltpu.SemaphoreType.DMA((1,))],
        specs=[ANY, HBM],
        out_specs=[HBM],
        aliases={1: 0},
    )
    return out


def solution(mesh):
    spec = P("gx", "gy", None, None, None)
    return jax.shard_map(
        per_device, mesh=mesh, in_specs=(spec,) * 6, out_specs=spec, check_vma=False
    )
```

```python
import functools

import jax
import jax.numpy as jnp
from jax import lax
from jax.experimental import pallas as pl
from jax.experimental.pallas import tpu as pltpu
from jax.sharding import PartitionSpec as P

CHAINS = ((0, 0), (1, 0), (0, 1), (1, 1), (0, 2), (1, 2))
T1, U1, T2, U2, T3, U3 = range(6)
UNITS = 4
VMEM = pl.BlockSpec(memory_space=pltpu.VMEM)
ANY = pl.BlockSpec(memory_space=pl.ANY)
HBM = pl.BlockSpec(memory_space=pltpu.HBM)


def spot(chain):
    direction, number = CHAINS[chain]
    return 3 * direction + number


def feeds(chain):
    return range(min(chain + 1, UNITS))


UNIT_START = {U1: (0, 4), T2: (8, 8), T1: (14, 8), U2: (24, 8), T3: (40, 8), U3: (56, 8)}
VECTOR_ROWS = 96
ROWS = VECTOR_ROWS + 72
UP_ROWS = {(T2, U1): (0, 2), (T3, U1): (4, 4), (T3, U2): (6, 4)}
DOWN_ROWS = {(U1, T1): (0, 2), (U2, T1): (4, 4), (U2, T2): (6, 4), (U3, T1): (12, 4), (U3, T2): (14, 4)}
LAST_UNITS = 24
LAST_ROWS = VECTOR_ROWS // 2 + LAST_UNITS


def vector_row(chain, a):
    return (2 * spot(chain) + a) * 8


def unit_row(chain, a):
    start, step = UNIT_START[chain]
    return VECTOR_ROWS + start + step * a


def unit_count(chain):
    return 2 * len(feeds(chain))


def half_of():
    top = lax.axis_size("gy") // 2
    flip = jnp.where(jnp.bitwise_and(lax.axis_index("gy"), top) == 0, 0, 1)
    return jnp.bitwise_xor(lax.axis_index("gx"), flip)


def keep_record(ref, values, chains=range(6)):
    for chain in chains:
        for a in (0, 1):
            carries, units = values[chain][a]
            ref[pl.ds(vector_row(chain, a), 8), :] = carries
            count = unit_count(chain)
            ref[pl.ds(unit_row(chain, a), count), :] = units[:count]


def spread(ref, row, count):
    return ref[pl.ds(row, count, stride=0), :]


def call(kernel, outs, ins, scratch=(), specs=None, out_specs=None, aliases={}):
    return pl.pallas_call(
        kernel,
        out_shape=[jax.ShapeDtypeStruct(s, jnp.float32) for s in outs],
        in_specs=specs or [VMEM] * len(ins),
        out_specs=out_specs or [VMEM] * len(outs),
        scratch_shapes=list(scratch),
        input_output_aliases=aliases,
        compiler_params=pltpu.CompilerParams(vmem_limit_bytes=8 << 20),
    )(*ins)


def pack_kernel(half, vectors, away, krylov, inverse, back, front, left, right, out, sems):
    core, part = lax.axis_index("gx"), half_of()
    position = 1 - part if away else part
    lanes = pl.ds(pl.multiple_of(position * half, half), half)
    base = (0, vectors, vectors + 2, vectors + 4, vectors + 6)

    def copy(ref, number):
        target = out.at[:, pl.ds(base[number], ref.shape[2])]
        return pltpu.make_async_copy(ref.at[0, :, :, :, lanes], target, sems.at[number])

    plan = [copy(ref, number) for number, ref in enumerate((krylov, inverse, left, right))]
    for one in plan:
        one.start()
    for own, ref in ((0, front), (1, back)):

        @pl.when(core == own)
        def _():
            one = copy(ref, 4)
            one.start()
            one.wait()

    for one in plan:
        one.wait()


def combine(ref, place, state):
    out = []
    for a in (0, 1):
        left, right = (spread(ref, place(a, b), 8) for b in (0, 1))
        out.append([left * x + right * y for x, y in zip(state[0], state[1])])
    return out


def add(x, y):
    return [[p + q for p, q in zip(s, t)] for s, t in zip(x, y)]


FORWARD, BACKWARD, ACROSS = range(3)


def make_maps(lines, vectors, data, maps):
    pitch = 2 * vectors + 16

    def block(number):
        start = 2 * vectors + 4 * number
        return [[data[pl.ds(start + 2 * a + b, lines, stride=pitch), :] for b in (0, 1)] for a in (0, 1)]

    inverse = block(0)
    for number in (FORWARD, BACKWARD, ACROSS):
        coupling = block(1 + number)
        for a in (0, 1):
            for b in (0, 1):
                value = -(inverse[a][0] * coupling[0][b] + inverse[a][1] * coupling[1][b])
                maps[pl.ds((4 * number + 2 * a + b) * lines, lines), :] = value


def mapped(lines, maps, number, line, state):
    return combine(maps, lambda a, b: (4 * number + 2 * a + b) * lines + line, state)


def scaled(vectors, data, line):
    start = line * (2 * vectors + 16)
    source = [[data[pl.ds(start + a, vectors, stride=2), :]] for a in (0, 1)]
    got = combine(data, lambda a, b: start + 2 * vectors + 2 * a + b, source)
    return [[s[0], jnp.zeros((8, 128), jnp.float32)] for s in got]


def unit(chain):
    row = lax.broadcasted_iota(jnp.int32, (8, 128), 0)
    none = jnp.zeros((8, 128), jnp.float32)
    one = [jnp.where(row == 2 * chain + a, 1.0, 0.0) if chain < UNITS else none for a in (0, 1)]
    return [[none, one[a]] for a in (0, 1)]


def sweep_plane(lines, maps, chain, source, leaving):
    state, states = unit(chain), []
    for line in range(lines):
        state = add(source(line), mapped(lines, maps, FORWARD, line, state))
        states.append(state)
    leaving[chain] = state
    state, result = unit(chain + 1), [None] * lines
    for line in reversed(range(lines)):
        state = add(states[line], mapped(lines, maps, BACKWARD, line, state))
        result[line] = state
    leaving[chain + 1] = state
    return result


def state_rows(line, a, part):
    return pl.ds((2 * line + a) * (8 + 2 * UNITS) + 8 * part, 8)


def early_kernel(lines, vectors, keep, swept, edge, maps):
    make_maps(lines, vectors, keep, maps)

    @pl.when(lax.axis_index("gx") == 0)
    def _():
        leaving = [None] * 6
        result = sweep_plane(lines, maps, T1, lambda line: scaled(vectors, keep, line), leaving)
        keep_record(edge, leaving, (T1, U1))
        for line in range(lines):
            for a in (0, 1):
                for part in (0, 1):
                    swept[state_rows(line, a, part), :] = result[line][a][part]


def local_kernel(lines, vectors, keep, recv, swept, early, own_maps, edge, first, second, low, other_maps):
    make_maps(lines, vectors, recv, other_maps)
    for own in (0, 1):

        @pl.when(lax.axis_index("gx") == own)
        def _():
            leaving = [None] * 6
            maps = (other_maps, own_maps) if own else (own_maps, other_maps)
            if own == 0:
                swept_low = [
                    [[swept[state_rows(line, a, part), :] for part in (0, 1)] for a in (0, 1)] for line in range(lines)
                ]
                for chain in (T1, U1):
                    leaving[chain] = [
                        [early[pl.ds(vector_row(chain, a), 8), :], early[pl.ds(unit_row(chain, a), 8), :]] for a in (0, 1)
                    ]
            else:
                swept_low = sweep_plane(lines, maps[0], T1, lambda line: scaled(vectors, recv, line), leaving)
            high_data = keep if own else recv
            swept_high = sweep_plane(
                lines,
                maps[1],
                T2,
                lambda line: add(scaled(vectors, high_data, line), mapped(lines, maps[1], ACROSS, line, swept_low[line])),
                leaving,
            )
            fixed = sweep_plane(
                lines, maps[0], T3, lambda line: mapped(lines, maps[0], ACROSS, line, swept_high[line]), leaving
            )
            keep_record(edge, leaving)
            for line in range(lines):
                total = add(swept_low[line], fixed[line])
                for a in (0, 1):
                    low[pl.ds((2 * line + a) * 8, 8), :] = swept_low[line][a][1]
                    for part in (0, 1):
                        first[state_rows(line, a, part), :] = total[a][part]
                        second[state_rows(line, a, part), :] = swept_high[line][a][part]


def times(ref, row, step, state):
    out = []
    for a in (0, 1):
        left, right = spread(ref, row + step * a, 8), spread(ref, row + step * a + 1, 8)
        out.append([left * x + right * y for x, y in zip(state[0], state[1])])
    return out


def response(ref, to, frm, state):
    if frm >= UNITS:
        to, frm = to - UNITS, frm - UNITS
    start, step = UNIT_START[to]
    return times(ref, VECTOR_ROWS + start + 2 * frm, step, state)


def total(first, *others):
    for other in others:
        first = [[p + q for p, q in zip(s, t)] for s, t in zip(first, other)]
    return first


def merge_kernel(bit, last, mine, other, edge, mids, lower, upper, *pair):
    is_low = jnp.bitwise_and(lax.axis_index("gy"), bit) == 0
    x, y = mine[...], other[...]
    lower[...] = jnp.where(is_low, x, y)
    upper[...] = jnp.where(is_low, y, x)
    row = lax.broadcasted_iota(jnp.int32, (8, 128), 0)
    up = jnp.bitwise_and(row, 2) == 0

    def base(ref, chain, keep_up):
        wanted = (up if keep_up else ~up) & (row < unit_count(chain))
        out = []
        for a in (0, 1):
            units = ref[pl.ds(unit_row(chain, a), 8), :]
            out.append([ref[pl.ds(vector_row(chain, a), 8), :], jnp.where(wanted, units, 0.0)])
        return out

    low = functools.partial(response, lower)
    high = functools.partial(response, upper)
    m = [None] * 6
    m[T1] = base(lower, T1, True)
    m[U1] = total(base(upper, U1, False), high(U1, T1, m[T1]))
    m[T2] = total(base(lower, T2, True), low(T2, U1, m[U1]))
    m[U2] = total(base(upper, U2, False), high(U2, T1, m[T1]), high(U2, T2, m[T2]))
    m[T3] = total(base(lower, T3, True), low(T3, U1, m[U1]), low(T3, U2, m[U2]))
    m[U3] = total(base(upper, U3, False), high(U3, T1, m[T1]), high(U3, T2, m[T2]), high(U3, T3, m[T3]))
    e = [None] * 6
    for chain in range(6):
        ref, of = (upper, high) if CHAINS[chain][0] == 0 else (lower, low)
        through = [c for c in range(chain + 1) if CHAINS[c][0] == CHAINS[chain][0]]
        e[chain] = total(base(ref, chain, CHAINS[chain][0] == 1), *(of(chain, c, m[c]) for c in through))
    keep_record(mids, m)
    if not last:
        keep_record(edge, e)
        return
    next_low = jnp.bitwise_and(lax.axis_index("gy"), 2 * bit) == 0
    for chain in (T1, T2, T3):
        for a in (0, 1):
            place = pl.ds(vector_row(chain, a), 8)
            edge[place, :] = jnp.where(next_low, e[chain][a][0], e[chain + 1][a][0])
    for ref, table in zip(pair, (UP_ROWS, DOWN_ROWS)):
        ref[...] = jnp.zeros_like(ref)
        for (to, frm), (start, step) in table.items():
            for a in (0, 1):
                ref[pl.ds(start + step * a, 2), :] = e[to][a][1][2 * frm : 2 * frm + 2]
    units = pl.ds(VECTOR_ROWS // 2, LAST_UNITS)
    edge[units, :] = jnp.where(next_low, pair[0][...], pair[1][...])


def compose_kernel(lines, levels, *refs):
    mids, (first, second, low, own, away) = refs[: levels - 1], refs[levels - 1 :]
    place, core = lax.axis_index("gy"), lax.axis_index("gx")
    row = lax.broadcasted_iota(jnp.int32, (8, 128), 0)
    none = jnp.zeros((8, 128), jnp.float32)
    in_low = jnp.bitwise_and(place, 1 << (levels - 1)) == 0

    def select(condition, x, y):
        return [[jnp.where(condition, p, q) for p, q in zip(s, t)] for s, t in zip(x, y)]

    enters = []
    for direction, number in CHAINS:
        one = [jnp.where(row == 2 * number + a, 1.0, 0.0) for a in (0, 1)]
        here = in_low if direction else ~in_low
        enters.append([[none, jnp.where(here, one[a], 0.0)] for a in (0, 1)])
    for level in reversed(range(levels - 1)):
        ref = mids[level]
        m = []
        for chain in range(6):
            base = [[ref[pl.ds(vector_row(chain, a), 8), :], none] for a in (0, 1)]
            terms = [response(ref, chain, c, enters[c]) for c in feeds(chain)]
            if chain >= UNITS:
                terms += [response(ref, chain, c, enters[c]) for c in range(UNITS, chain + 1)]
            m.append(total(base, *terms))
        is_low = jnp.bitwise_and(place, 1 << level) == 0
        enters = [
            select(is_low, enters[c], m[c]) if CHAINS[c][0] == 0 else select(is_low, m[c], enters[c])
            for c in range(6)
        ]

    width = 8 + 2 * UNITS
    units = [(c, c) for c in range(UNITS)]
    for line in range(lines):
        for a in (0, 1):
            start = (2 * line + a) * width
            planes = []
            for source, extra in ((first, [(T1, T3), (U1, U3)]), (second, [])):
                value = [source[pl.ds(start, 8), :], none]
                pairs = [(source, start + 8, pair) for pair in units]
                pairs += [(low, (2 * line + a) * 8, pair) for pair in extra]
                for ref, begin, (column, chain) in pairs:
                    for b in (0, 1):
                        factor = spread(ref, begin + 2 * column + b, 8)
                        value = [v + factor * e for v, e in zip(value, enters[chain][b])]
                planes.append(value)
            for part in (0, 1):
                mine, other = planes[0][part], planes[1][part]
                own[state_rows(line, a, part), :] = jnp.where(core == 0, mine, other)
                away[state_rows(line, a, part), :] = jnp.where(core == 0, other, mine)


def apply_map(lines, ref, entry, target):
    width = 8 + 2 * UNITS
    for line in range(lines):
        for a in (0, 1):
            start = (2 * line + a) * width
            value = ref[pl.ds(start, 8), :]
            for number in range(3):
                for b in (0, 1):
                    value = value + spread(ref, start + 8 + 2 * number + b, 8) * entry[number][b]
            target[pl.ds(line * 16 + a, 8, stride=2), :] = value


def finish_kernel(levels, mine, other, entry, ups, downs):
    is_low = jnp.bitwise_and(lax.axis_index("gy"), 1 << (levels - 1)) == 0
    x, y = mine[...], other[...]
    ups[...] = jnp.where(is_low, x, y)
    downs[...] = jnp.where(is_low, y, x)

    def base(ref, chain, first_chain):
        skip = vector_row(first_chain, 0)
        return [[ref[pl.ds(vector_row(chain, a) - skip, 8), :]] for a in (0, 1)]

    def up(to, frm, state):
        start, step = UP_ROWS[to, frm]
        return times(ups, VECTOR_ROWS // 2 + start, step, state)

    def down(to, frm, state):
        if frm >= UNITS:
            to, frm = to - UNITS, frm - UNITS
        start, step = DOWN_ROWS[to, frm]
        return times(downs, VECTOR_ROWS // 2 + start, step, state)

    m = [None] * 6
    m[T1] = base(ups, T1, T1)
    m[U1] = total(base(downs, U1, U1), down(U1, T1, m[T1]))
    m[T2] = total(base(ups, T2, T1), up(T2, U1, m[U1]))
    m[U2] = total(base(downs, U2, U1), down(U2, T1, m[T1]), down(U2, T2, m[T2]))
    m[T3] = total(base(ups, T3, T1), up(T3, U1, m[U1]), up(T3, U2, m[U2]))
    m[U3] = total(base(downs, U3, U1), down(U3, T1, m[T1]), down(U3, T2, m[T2]), down(U3, T3, m[T3]))
    enters = [
        [jnp.where(is_low, m[2 * number + 1][b][0], m[2 * number][b][0]) for b in (0, 1)] for number in range(3)
    ]
    for number in range(3):
        for b in (0, 1):
            entry[pl.ds((2 * number + b) * 8, 8), :] = enters[number][b]


def own_kernel(lines, entry, own, kept):
    enters = [[entry[pl.ds((2 * number + b) * 8, 8), :] for b in (0, 1)] for number in range(3)]
    apply_map(lines, own, enters, kept)


def part_copy(half, position, value, out, sem):
    lanes = pl.ds(pl.multiple_of(position * half, half), half)
    return pltpu.make_async_copy(value, out.at[0, :, :, :, lanes], sem)


def store_kernel(half, kept, out, sem):
    one = part_copy(half, half_of(), kept, out, sem.at[0])
    one.start()
    one.wait()


def last_kernel(half, got, before, out, sem):
    one = part_copy(half, 1 - half_of(), got, out, sem.at[0])
    one.start()
    one.wait()


def per_device(krylov, inverse, back, front, left, right):
    _, lines, vectors, _, cells = krylov.shape
    count = lax.axis_size("gy")
    levels = count.bit_length() - 1
    half = cells // 2
    width = vectors + 2 * UNITS
    assert lax.axis_size("gx") == 2 and count == 1 << levels and levels > 1
    assert vectors == 8 and half == 128
    swap = [(0, 1), (1, 0)]

    arguments = [pltpu.with_memory_space_constraint(x, pltpu.HBM) for x in (krylov, inverse, back, front, left, right)]

    def pack(away):
        (out,) = call(
            functools.partial(pack_kernel, half, vectors, away),
            [(lines, vectors + 8, 2, half)],
            arguments,
            [pltpu.SemaphoreType.DMA((5,))],
            specs=[HBM] * 6,
        )
        return out.reshape(-1, half)

    recv = lax.ppermute(pack(True), "gx", swap)
    keep = pack(False)
    swept, early, own_maps = call(
        functools.partial(early_kernel, lines, vectors),
        [(2 * lines * width, half), (ROWS, half), (12 * lines, half)],
        (keep,),
    )
    edge, first, second, low = call(
        functools.partial(local_kernel, lines, vectors),
        [(ROWS, half), (2 * lines * width, half), (2 * lines * width, half), (2 * lines * 8, half)],
        (keep, recv, swept, early, own_maps),
        [pltpu.VMEM((12 * lines, half), jnp.float32)],
    )
    mids = []
    for level in range(levels - 1):
        got = lax.ppermute(edge, "gy", [(j, j ^ (1 << level)) for j in range(count)])
        last = level == levels - 2
        edge, mid = call(
            functools.partial(merge_kernel, 1 << level, last),
            [(LAST_ROWS if last else ROWS, half), (ROWS, half)],
            (edge, got),
            [pltpu.VMEM((ROWS, half), jnp.float32)] * 2 + [pltpu.VMEM((LAST_UNITS, half), jnp.float32)] * (2 * last),
        )
        mids.append(mid)
    across = [(core * count + j, (1 - core) * count + (j ^ (count // 2))) for core in (0, 1) for j in range(count)]
    got = lax.ppermute(edge, ("gx", "gy"), across)
    own, away = call(
        functools.partial(compose_kernel, lines, levels), [(2 * lines * width, half)] * 2, (*mids, first, second, low)
    )
    away = lax.ppermute(away, "gx", swap)
    (entry,) = call(
        functools.partial(finish_kernel, levels),
        [(VECTOR_ROWS // 2, half)],
        (edge, got),
        [pltpu.VMEM((LAST_ROWS, half), jnp.float32)] * 2,
    )
    got_entry = lax.ppermute(entry, "gx", swap)

    def plane_half(carries, ref):
        (value,) = call(functools.partial(own_kernel, lines), [(lines * 16, half)], (carries, ref))
        return value.reshape(lines, vectors, 2, half)

    kept = plane_half(entry, own)
    (out,) = call(
        functools.partial(store_kernel, half),
        [krylov.shape],
        [kept],
        [pltpu.SemaphoreType.DMA((1,))],
        specs=[ANY],
        out_specs=[HBM],
    )
    (out,) = call(
        functools.partial(last_kernel, half),
        [krylov.shape],
        [plane_half(got_entry, away), out],
        [pltpu.SemaphoreType.DMA((1,))],
        specs=[ANY, HBM],
        out_specs=[HBM],
        aliases={1: 0},
    )
    return out


def solution(mesh):
    spec = P("gx", "gy", None, None, None)
    return jax.shard_map(
        per_device, mesh=mesh, in_specs=(spec,) * 6, out_specs=spec, check_vma=False
    )
```

```python
import functools

import jax
import jax.numpy as jnp
from jax import lax
from jax.experimental import pallas as pl
from jax.experimental.pallas import tpu as pltpu
from jax.sharding import PartitionSpec as P

CHAINS = ((0, 0), (1, 0), (0, 1), (1, 1), (0, 2), (1, 2))
T1, U1, T2, U2, T3, U3 = range(6)
UNITS = 4
VMEM = pl.BlockSpec(memory_space=pltpu.VMEM)
ANY = pl.BlockSpec(memory_space=pl.ANY)
HBM = pl.BlockSpec(memory_space=pltpu.HBM)


def spot(chain):
    direction, number = CHAINS[chain]
    return 3 * direction + number


def feeds(chain):
    return range(min(chain + 1, UNITS))


UNIT_START = {U1: (0, 4), T2: (8, 8), T1: (14, 8), U2: (24, 8), T3: (40, 8), U3: (56, 8)}
VECTOR_ROWS = 96
ROWS = VECTOR_ROWS + 72
UP_ROWS = {(T2, U1): (0, 2), (T3, U1): (4, 4), (T3, U2): (6, 4)}
DOWN_ROWS = {(U1, T1): (0, 2), (U2, T1): (4, 4), (U2, T2): (6, 4), (U3, T1): (12, 4), (U3, T2): (14, 4)}
LAST_UNITS = 24
LAST_ROWS = VECTOR_ROWS // 2 + LAST_UNITS


def vector_row(chain, a):
    return (2 * spot(chain) + a) * 8


def unit_row(chain, a):
    start, step = UNIT_START[chain]
    return VECTOR_ROWS + start + step * a


def unit_count(chain):
    return 2 * len(feeds(chain))


def half_of():
    top = lax.axis_size("gy") // 2
    flip = jnp.where(jnp.bitwise_and(lax.axis_index("gy"), top) == 0, 0, 1)
    return jnp.bitwise_xor(lax.axis_index("gx"), flip)


def keep_record(ref, values, chains=range(6)):
    for chain in chains:
        for a in (0, 1):
            carries, units = values[chain][a]
            ref[pl.ds(vector_row(chain, a), 8), :] = carries
            count = unit_count(chain)
            ref[pl.ds(unit_row(chain, a), count), :] = units[:count]


def spread(ref, row, count):
    return ref[pl.ds(row, count, stride=0), :]


def call(kernel, outs, ins, scratch=(), specs=None, out_specs=None, aliases={}):
    return pl.pallas_call(
        kernel,
        out_shape=[jax.ShapeDtypeStruct(s, jnp.float32) for s in outs],
        in_specs=specs or [VMEM] * len(ins),
        out_specs=out_specs or [VMEM] * len(outs),
        scratch_shapes=list(scratch),
        input_output_aliases=aliases,
        compiler_params=pltpu.CompilerParams(vmem_limit_bytes=8 << 20),
    )(*ins)


def pack_kernel(half, vectors, away, krylov, inverse, back, front, left, right, out, sems):
    core, part = lax.axis_index("gx"), half_of()
    position = 1 - part if away else part
    lanes = pl.ds(pl.multiple_of(position * half, half), half)
    base = (0, vectors, vectors + 2, vectors + 4, vectors + 6)

    def copy(ref, number):
        target = out.at[:, pl.ds(base[number], ref.shape[2])]
        return pltpu.make_async_copy(ref.at[0, :, :, :, lanes], target, sems.at[number])

    plan = [copy(ref, number) for number, ref in enumerate((krylov, inverse, left, right))]
    for one in plan:
        one.start()
    for own, ref in ((0, front), (1, back)):

        @pl.when(core == own)
        def _():
            one = copy(ref, 4)
            one.start()
            one.wait()

    for one in plan:
        one.wait()


def combine(ref, place, state):
    out = []
    for a in (0, 1):
        left, right = (spread(ref, place(a, b), 8) for b in (0, 1))
        out.append([left * x + right * y for x, y in zip(state[0], state[1])])
    return out


def add(x, y):
    return [[p + q for p, q in zip(s, t)] + t[len(s) :] for s, t in zip(x, y)]


FORWARD, BACKWARD, ACROSS = range(3)


def make_maps(lines, vectors, data, maps):
    pitch = 2 * vectors + 16

    def block(number):
        start = 2 * vectors + 4 * number
        return [[data[pl.ds(start + 2 * a + b, lines, stride=pitch), :] for b in (0, 1)] for a in (0, 1)]

    inverse = block(0)
    for number in (FORWARD, BACKWARD, ACROSS):
        coupling = block(1 + number)
        for a in (0, 1):
            for b in (0, 1):
                value = -(inverse[a][0] * coupling[0][b] + inverse[a][1] * coupling[1][b])
                maps[pl.ds((4 * number + 2 * a + b) * lines, lines), :] = value


def mapped(lines, maps, number, line, state):
    return combine(maps, lambda a, b: (4 * number + 2 * a + b) * lines + line, state)


def scaled(vectors, data, line):
    start = line * (2 * vectors + 16)
    source = [[data[pl.ds(start + a, vectors, stride=2), :]] for a in (0, 1)]
    return combine(data, lambda a, b: start + 2 * vectors + 2 * a + b, source)


def unit(chain):
    row = lax.broadcasted_iota(jnp.int32, (8, 128), 0)
    none = jnp.zeros((8, 128), jnp.float32)
    one = [jnp.where(row == 2 * chain + a, 1.0, 0.0) if chain < UNITS else none for a in (0, 1)]
    return [[none, one[a]] for a in (0, 1)]


def sweep_plane(lines, maps, chain, source, leaving):
    state, states = unit(chain), []
    for line in range(lines):
        first = line == 0 and chain >= UNITS
        state = source(line) if first else add(source(line), mapped(lines, maps, FORWARD, line, state))
        states.append(state)
    leaving[chain] = state
    state, result = unit(chain + 1), [None] * lines
    for line in reversed(range(lines)):
        first = line == lines - 1 and chain + 1 >= UNITS
        state = states[line] if first else add(states[line], mapped(lines, maps, BACKWARD, line, state))
        result[line] = state
    leaving[chain + 1] = state
    return result


def state_rows(line, a, part):
    return pl.ds((2 * line + a) * (8 + 2 * UNITS) + 8 * part, 8)


def early_kernel(lines, vectors, keep, swept, edge, maps):
    make_maps(lines, vectors, keep, maps)

    @pl.when(lax.axis_index("gx") == 0)
    def _():
        leaving = [None] * 6
        result = sweep_plane(lines, maps, T1, lambda line: scaled(vectors, keep, line), leaving)
        keep_record(edge, leaving, (T1, U1))
        for line in range(lines):
            for a in (0, 1):
                for part in (0, 1):
                    swept[state_rows(line, a, part), :] = result[line][a][part]


def local_kernel(lines, vectors, keep, recv, swept, early, own_maps, edge, first, second, low, other_maps):
    make_maps(lines, vectors, recv, other_maps)
    for own in (0, 1):

        @pl.when(lax.axis_index("gx") == own)
        def _():
            leaving = [None] * 6
            maps = (other_maps, own_maps) if own else (own_maps, other_maps)
            if own == 0:
                swept_low = [
                    [[swept[state_rows(line, a, part), :] for part in (0, 1)] for a in (0, 1)] for line in range(lines)
                ]
                for chain in (T1, U1):
                    leaving[chain] = [
                        [early[pl.ds(vector_row(chain, a), 8), :], early[pl.ds(unit_row(chain, a), 8), :]] for a in (0, 1)
                    ]
            else:
                swept_low = sweep_plane(lines, maps[0], T1, lambda line: scaled(vectors, recv, line), leaving)
            high_data = keep if own else recv
            swept_high = sweep_plane(
                lines,
                maps[1],
                T2,
                lambda line: add(scaled(vectors, high_data, line), mapped(lines, maps[1], ACROSS, line, swept_low[line])),
                leaving,
            )
            fixed = sweep_plane(
                lines, maps[0], T3, lambda line: mapped(lines, maps[0], ACROSS, line, swept_high[line]), leaving
            )
            keep_record(edge, leaving)
            for line in range(lines):
                total = add(swept_low[line], fixed[line])
                for a in (0, 1):
                    low[pl.ds((2 * line + a) * 8, 8), :] = swept_low[line][a][1]
                    for part in (0, 1):
                        first[state_rows(line, a, part), :] = total[a][part]
                        second[state_rows(line, a, part), :] = swept_high[line][a][part]


def times(ref, row, step, state):
    out = []
    for a in (0, 1):
        left, right = spread(ref, row + step * a, 8), spread(ref, row + step * a + 1, 8)
        out.append([left * x + right * y for x, y in zip(state[0], state[1])])
    return out


def response(ref, to, frm, state):
    if frm >= UNITS:
        to, frm = to - UNITS, frm - UNITS
    start, step = UNIT_START[to]
    return times(ref, VECTOR_ROWS + start + 2 * frm, step, state)


def total(first, *others):
    for other in others:
        first = [[p + q for p, q in zip(s, t)] for s, t in zip(first, other)]
    return first


def merge_kernel(bit, last, mine, other, edge, mids, *pair):
    is_low = jnp.bitwise_and(lax.axis_index("gy"), bit) == 0
    for low_side in (True, False):

        @pl.when(is_low if low_side else ~is_low)
        def _():
            lower, upper = (mine, other) if low_side else (other, mine)
            merge_records(bit, last, lower, upper, edge, mids, *pair)


def merge_records(bit, last, lower, upper, edge, mids, *pair):
    row = lax.broadcasted_iota(jnp.int32, (8, 128), 0)
    up = jnp.bitwise_and(row, 2) == 0

    def base(ref, chain, keep_up):
        wanted = (up if keep_up else ~up) & (row < unit_count(chain))
        out = []
        for a in (0, 1):
            units = ref[pl.ds(unit_row(chain, a), 8), :]
            out.append([ref[pl.ds(vector_row(chain, a), 8), :], jnp.where(wanted, units, 0.0)])
        return out

    low = functools.partial(response, lower)
    high = functools.partial(response, upper)
    m = [None] * 6
    m[T1] = base(lower, T1, True)
    m[U1] = total(base(upper, U1, False), high(U1, T1, m[T1]))
    m[T2] = total(base(lower, T2, True), low(T2, U1, m[U1]))
    m[U2] = total(base(upper, U2, False), high(U2, T1, m[T1]), high(U2, T2, m[T2]))
    m[T3] = total(base(lower, T3, True), low(T3, U1, m[U1]), low(T3, U2, m[U2]))
    m[U3] = total(base(upper, U3, False), high(U3, T1, m[T1]), high(U3, T2, m[T2]), high(U3, T3, m[T3]))
    e = [None] * 6
    for chain in range(6):
        ref, of = (upper, high) if CHAINS[chain][0] == 0 else (lower, low)
        through = [c for c in range(chain + 1) if CHAINS[c][0] == CHAINS[chain][0]]
        e[chain] = total(base(ref, chain, CHAINS[chain][0] == 1), *(of(chain, c, m[c]) for c in through))
    keep_record(mids, m)
    if not last:
        keep_record(edge, e)
        return
    next_low = jnp.bitwise_and(lax.axis_index("gy"), 2 * bit) == 0
    for chain in (T1, T2, T3):
        for a in (0, 1):
            place = pl.ds(vector_row(chain, a), 8)
            edge[place, :] = jnp.where(next_low, e[chain][a][0], e[chain + 1][a][0])
    for ref, table in zip(pair, (UP_ROWS, DOWN_ROWS)):
        ref[...] = jnp.zeros_like(ref)
        for (to, frm), (start, step) in table.items():
            for a in (0, 1):
                ref[pl.ds(start + step * a, 2), :] = e[to][a][1][2 * frm : 2 * frm + 2]
    units = pl.ds(VECTOR_ROWS // 2, LAST_UNITS)
    edge[units, :] = jnp.where(next_low, pair[0][...], pair[1][...])


def compose_kernel(lines, levels, *refs):
    mids, (first, second, low, own, away) = refs[: levels - 1], refs[levels - 1 :]
    place, core = lax.axis_index("gy"), lax.axis_index("gx")
    row = lax.broadcasted_iota(jnp.int32, (8, 128), 0)
    none = jnp.zeros((8, 128), jnp.float32)
    in_low = jnp.bitwise_and(place, 1 << (levels - 1)) == 0

    def select(condition, x, y):
        return [[jnp.where(condition, p, q) for p, q in zip(s, t)] for s, t in zip(x, y)]

    enters = []
    for direction, number in CHAINS:
        one = [jnp.where(row == 2 * number + a, 1.0, 0.0) for a in (0, 1)]
        here = in_low if direction else ~in_low
        enters.append([[none, jnp.where(here, one[a], 0.0)] for a in (0, 1)])
    for level in reversed(range(levels - 1)):
        ref = mids[level]
        m = []
        for chain in range(6):
            base = [[ref[pl.ds(vector_row(chain, a), 8), :], none] for a in (0, 1)]
            terms = [response(ref, chain, c, enters[c]) for c in feeds(chain)]
            if chain >= UNITS:
                terms += [response(ref, chain, c, enters[c]) for c in range(UNITS, chain + 1)]
            m.append(total(base, *terms))
        is_low = jnp.bitwise_and(place, 1 << level) == 0
        enters = [
            select(is_low, enters[c], m[c]) if CHAINS[c][0] == 0 else select(is_low, m[c], enters[c])
            for c in range(6)
        ]

    width = 8 + 2 * UNITS
    units = [(c, c) for c in range(UNITS)]
    for line in range(lines):
        for a in (0, 1):
            start = (2 * line + a) * width
            planes = []
            for source, extra in ((first, [(T1, T3), (U1, U3)]), (second, [])):
                value = [source[pl.ds(start, 8), :], none]
                pairs = [(source, start + 8, pair) for pair in units]
                pairs += [(low, (2 * line + a) * 8, pair) for pair in extra]
                for ref, begin, (column, chain) in pairs:
                    for b in (0, 1):
                        factor = spread(ref, begin + 2 * column + b, 8)
                        value = [v + factor * e for v, e in zip(value, enters[chain][b])]
                planes.append(value)
            for part in (0, 1):
                mine, other = planes[0][part], planes[1][part]
                own[state_rows(line, a, part), :] = jnp.where(core == 0, mine, other)
                away[state_rows(line, a, part), :] = jnp.where(core == 0, other, mine)


def apply_map(lines, ref, entry, target):
    width = 8 + 2 * UNITS
    for line in range(lines):
        for a in (0, 1):
            start = (2 * line + a) * width
            value = ref[pl.ds(start, 8), :]
            for number in range(3):
                for b in (0, 1):
                    value = value + spread(ref, start + 8 + 2 * number + b, 8) * entry[number][b]
            target[pl.ds(line * 16 + a, 8, stride=2), :] = value


def finish_kernel(levels, mine, other, entry, ups, downs):
    is_low = jnp.bitwise_and(lax.axis_index("gy"), 1 << (levels - 1)) == 0
    x, y = mine[...], other[...]
    ups[...] = jnp.where(is_low, x, y)
    downs[...] = jnp.where(is_low, y, x)

    def base(ref, chain, first_chain):
        skip = vector_row(first_chain, 0)
        return [[ref[pl.ds(vector_row(chain, a) - skip, 8), :]] for a in (0, 1)]

    def up(to, frm, state):
        start, step = UP_ROWS[to, frm]
        return times(ups, VECTOR_ROWS // 2 + start, step, state)

    def down(to, frm, state):
        if frm >= UNITS:
            to, frm = to - UNITS, frm - UNITS
        start, step = DOWN_ROWS[to, frm]
        return times(downs, VECTOR_ROWS // 2 + start, step, state)

    m = [None] * 6
    m[T1] = base(ups, T1, T1)
    m[U1] = total(base(downs, U1, U1), down(U1, T1, m[T1]))
    m[T2] = total(base(ups, T2, T1), up(T2, U1, m[U1]))
    m[U2] = total(base(downs, U2, U1), down(U2, T1, m[T1]), down(U2, T2, m[T2]))
    m[T3] = total(base(ups, T3, T1), up(T3, U1, m[U1]), up(T3, U2, m[U2]))
    m[U3] = total(base(downs, U3, U1), down(U3, T1, m[T1]), down(U3, T2, m[T2]), down(U3, T3, m[T3]))
    enters = [
        [jnp.where(is_low, m[2 * number + 1][b][0], m[2 * number][b][0]) for b in (0, 1)] for number in range(3)
    ]
    for number in range(3):
        for b in (0, 1):
            entry[pl.ds((2 * number + b) * 8, 8), :] = enters[number][b]


def own_kernel(lines, entry, own, kept):
    enters = [[entry[pl.ds((2 * number + b) * 8, 8), :] for b in (0, 1)] for number in range(3)]
    apply_map(lines, own, enters, kept)


def part_copy(half, position, value, out, sem):
    lanes = pl.ds(pl.multiple_of(position * half, half), half)
    return pltpu.make_async_copy(value, out.at[0, :, :, :, lanes], sem)


def store_kernel(half, kept, out, sem):
    one = part_copy(half, half_of(), kept, out, sem.at[0])
    one.start()
    one.wait()


def last_kernel(half, got, before, out, sem):
    one = part_copy(half, 1 - half_of(), got, out, sem.at[0])
    one.start()
    one.wait()


def per_device(krylov, inverse, back, front, left, right):
    _, lines, vectors, _, cells = krylov.shape
    count = lax.axis_size("gy")
    levels = count.bit_length() - 1
    half = cells // 2
    width = vectors + 2 * UNITS
    assert lax.axis_size("gx") == 2 and count == 1 << levels and levels > 1
    assert vectors == 8 and half == 128
    swap = [(0, 1), (1, 0)]

    arguments = [pltpu.with_memory_space_constraint(x, pltpu.HBM) for x in (krylov, inverse, back, front, left, right)]

    def pack(away):
        (out,) = call(
            functools.partial(pack_kernel, half, vectors, away),
            [(lines, vectors + 8, 2, half)],
            arguments,
            [pltpu.SemaphoreType.DMA((5,))],
            specs=[HBM] * 6,
        )
        return out.reshape(-1, half)

    recv = lax.ppermute(pack(True), "gx", swap)
    keep = pack(False)
    swept, early, own_maps = call(
        functools.partial(early_kernel, lines, vectors),
        [(2 * lines * width, half), (ROWS, half), (12 * lines, half)],
        (keep,),
    )
    edge, first, second, low = call(
        functools.partial(local_kernel, lines, vectors),
        [(ROWS, half), (2 * lines * width, half), (2 * lines * width, half), (2 * lines * 8, half)],
        (keep, recv, swept, early, own_maps),
        [pltpu.VMEM((12 * lines, half), jnp.float32)],
    )
    mids = []
    for level in range(levels - 1):
        got = lax.ppermute(edge, "gy", [(j, j ^ (1 << level)) for j in range(count)])
        last = level == levels - 2
        edge, mid = call(
            functools.partial(merge_kernel, 1 << level, last),
            [(LAST_ROWS if last else ROWS, half), (ROWS, half)],
            (edge, got),
            [pltpu.VMEM((LAST_UNITS, half), jnp.float32)] * (2 * last),
        )
        mids.append(mid)
    across = [(core * count + j, (1 - core) * count + (j ^ (count // 2))) for core in (0, 1) for j in range(count)]
    got = lax.ppermute(edge, ("gx", "gy"), across)
    own, away = call(
        functools.partial(compose_kernel, lines, levels), [(2 * lines * width, half)] * 2, (*mids, first, second, low)
    )
    away = lax.ppermute(away, "gx", swap)
    (entry,) = call(
        functools.partial(finish_kernel, levels),
        [(VECTOR_ROWS // 2, half)],
        (edge, got),
        [pltpu.VMEM((LAST_ROWS, half), jnp.float32)] * 2,
    )
    got_entry = lax.ppermute(entry, "gx", swap)

    def plane_half(carries, ref):
        (value,) = call(functools.partial(own_kernel, lines), [(lines * 16, half)], (carries, ref))
        return value.reshape(lines, vectors, 2, half)

    kept = plane_half(entry, own)
    (out,) = call(
        functools.partial(store_kernel, half),
        [krylov.shape],
        [kept],
        [pltpu.SemaphoreType.DMA((1,))],
        specs=[ANY],
        out_specs=[HBM],
    )
    (out,) = call(
        functools.partial(last_kernel, half),
        [krylov.shape],
        [plane_half(got_entry, away), out],
        [pltpu.SemaphoreType.DMA((1,))],
        specs=[ANY, HBM],
        out_specs=[HBM],
        aliases={1: 0},
    )
    return out


def solution(mesh):
    spec = P("gx", "gy", None, None, None)
    return jax.shard_map(
        per_device, mesh=mesh, in_specs=(spec,) * 6, out_specs=spec, check_vma=False
    )
```

```python
import functools

import jax
import jax.numpy as jnp
from jax import lax
from jax.experimental import pallas as pl
from jax.experimental.pallas import tpu as pltpu
from jax.sharding import PartitionSpec as P

CHAINS = ((0, 0), (1, 0), (0, 1), (1, 1), (0, 2), (1, 2))
T1, U1, T2, U2, T3, U3 = range(6)
UNITS = 4
VMEM = pl.BlockSpec(memory_space=pltpu.VMEM)
ANY = pl.BlockSpec(memory_space=pl.ANY)
HBM = pl.BlockSpec(memory_space=pltpu.HBM)


def spot(chain):
    direction, number = CHAINS[chain]
    return 3 * direction + number


def feeds(chain):
    return range(min(chain + 1, UNITS))


UNIT_START = {U1: (0, 4), T2: (8, 8), T1: (14, 8), U2: (24, 8), T3: (40, 8), U3: (56, 8)}
VECTOR_ROWS = 96
ROWS = VECTOR_ROWS + 72
UP_ROWS = {(T2, U1): (0, 2), (T3, U1): (4, 4), (T3, U2): (6, 4)}
DOWN_ROWS = {(U1, T1): (0, 2), (U2, T1): (4, 4), (U2, T2): (6, 4), (U3, T1): (12, 4), (U3, T2): (14, 4)}
LAST_UNITS = 24
LAST_ROWS = VECTOR_ROWS // 2 + LAST_UNITS


def vector_row(chain, a):
    return (2 * spot(chain) + a) * 8


def unit_row(chain, a):
    start, step = UNIT_START[chain]
    return VECTOR_ROWS + start + step * a


def unit_count(chain):
    return 2 * len(feeds(chain))


def half_of():
    top = lax.axis_size("gy") // 2
    flip = jnp.where(jnp.bitwise_and(lax.axis_index("gy"), top) == 0, 0, 1)
    return jnp.bitwise_xor(lax.axis_index("gx"), flip)


def keep_record(ref, values, chains=range(6)):
    for chain in chains:
        for a in (0, 1):
            carries, units = values[chain][a]
            ref[pl.ds(vector_row(chain, a), 8), :] = carries
            count = unit_count(chain)
            ref[pl.ds(unit_row(chain, a), count), :] = units[:count]


def spread(ref, row, count):
    return ref[pl.ds(row, count, stride=0), :]


def call(kernel, outs, ins, scratch=(), specs=None, out_specs=None, aliases={}):
    return pl.pallas_call(
        kernel,
        out_shape=[jax.ShapeDtypeStruct(s, jnp.float32) for s in outs],
        in_specs=specs or [VMEM] * len(ins),
        out_specs=out_specs or [VMEM] * len(outs),
        scratch_shapes=list(scratch),
        input_output_aliases=aliases,
        compiler_params=pltpu.CompilerParams(vmem_limit_bytes=8 << 20),
    )(*ins)


def pack_kernel(half, vectors, away, krylov, inverse, back, front, left, right, out, sems):
    core, part = lax.axis_index("gx"), half_of()
    position = 1 - part if away else part
    lanes = pl.ds(pl.multiple_of(position * half, half), half)
    base = (0, vectors, vectors + 2, vectors + 4, vectors + 6)

    def copy(ref, number):
        target = out.at[:, pl.ds(base[number], ref.shape[2])]
        return pltpu.make_async_copy(ref.at[0, :, :, :, lanes], target, sems.at[number])

    plan = [copy(ref, number) for number, ref in enumerate((krylov, inverse, left, right))]
    for one in plan:
        one.start()
    for own, ref in ((0, front), (1, back)):

        @pl.when(core == own)
        def _():
            one = copy(ref, 4)
            one.start()
            one.wait()

    for one in plan:
        one.wait()


def combine(ref, place, state):
    out = []
    for a in (0, 1):
        left, right = (spread(ref, place(a, b), 8) for b in (0, 1))
        out.append([left * x + right * y for x, y in zip(state[0], state[1])])
    return out


def add(x, y):
    return [[p + q for p, q in zip(s, t)] + t[len(s) :] for s, t in zip(x, y)]


FORWARD, BACKWARD, ACROSS = range(3)


def make_maps(lines, vectors, data, maps):
    pitch = 2 * vectors + 16

    def block(number):
        start = 2 * vectors + 4 * number
        return [[data[pl.ds(start + 2 * a + b, lines, stride=pitch), :] for b in (0, 1)] for a in (0, 1)]

    inverse = block(0)
    for number in (FORWARD, BACKWARD, ACROSS):
        coupling = block(1 + number)
        for a in (0, 1):
            for b in (0, 1):
                value = -(inverse[a][0] * coupling[0][b] + inverse[a][1] * coupling[1][b])
                maps[pl.ds((4 * number + 2 * a + b) * lines, lines), :] = value


def mapped(lines, maps, number, line, state):
    return combine(maps, lambda a, b: (4 * number + 2 * a + b) * lines + line, state)


def scaled(vectors, data, line):
    start = line * (2 * vectors + 16)
    source = [[data[pl.ds(start + a, vectors, stride=2), :]] for a in (0, 1)]
    return combine(data, lambda a, b: start + 2 * vectors + 2 * a + b, source)


def unit(chain):
    row = lax.broadcasted_iota(jnp.int32, (8, 128), 0)
    none = jnp.zeros((8, 128), jnp.float32)
    one = [jnp.where(row == 2 * chain + a, 1.0, 0.0) if chain < UNITS else none for a in (0, 1)]
    return [[none, one[a]] for a in (0, 1)]


def sweep_plane(lines, maps, chain, source, leaving):
    state, states = unit(chain), []
    for line in range(lines):
        first = line == 0 and chain >= UNITS
        state = source(line) if first else add(source(line), mapped(lines, maps, FORWARD, line, state))
        states.append(state)
    leaving[chain] = state
    state, result = unit(chain + 1), [None] * lines
    for line in reversed(range(lines)):
        first = line == lines - 1 and chain + 1 >= UNITS
        state = states[line] if first else add(states[line], mapped(lines, maps, BACKWARD, line, state))
        result[line] = state
    leaving[chain + 1] = state
    return result


def state_rows(line, a, part):
    return pl.ds((2 * line + a) * (8 + 2 * UNITS) + 8 * part, 8)


def early_kernel(lines, vectors, keep, swept, edge, maps):
    make_maps(lines, vectors, keep, maps)

    @pl.when(lax.axis_index("gx") == 0)
    def _():
        leaving = [None] * 6
        result = sweep_plane(lines, maps, T1, lambda line: scaled(vectors, keep, line), leaving)
        keep_record(edge, leaving, (T1, U1))
        for line in range(lines):
            for a in (0, 1):
                for part in (0, 1):
                    swept[state_rows(line, a, part), :] = result[line][a][part]


def local_kernel(lines, vectors, keep, recv, swept, early, own_maps, edge, fixed_low, second, low, other_maps):
    make_maps(lines, vectors, recv, other_maps)
    for own in (0, 1):

        @pl.when(lax.axis_index("gx") == own)
        def _():
            leaving = [None] * 6
            maps = (other_maps, own_maps) if own else (own_maps, other_maps)
            if own == 0:
                swept_low = [
                    [[swept[state_rows(line, a, part), :] for part in (0, 1)] for a in (0, 1)] for line in range(lines)
                ]
                for chain in (T1, U1):
                    leaving[chain] = [
                        [early[pl.ds(vector_row(chain, a), 8), :], early[pl.ds(unit_row(chain, a), 8), :]] for a in (0, 1)
                    ]
            else:
                swept_low = sweep_plane(lines, maps[0], T1, lambda line: scaled(vectors, recv, line), leaving)
            high_data = keep if own else recv
            swept_high = sweep_plane(
                lines,
                maps[1],
                T2,
                lambda line: add(scaled(vectors, high_data, line), mapped(lines, maps[1], ACROSS, line, swept_low[line])),
                leaving,
            )
            fixed = sweep_plane(
                lines, maps[0], T3, lambda line: mapped(lines, maps[0], ACROSS, line, swept_high[line]), leaving
            )
            keep_record(edge, leaving)
            for line in range(lines):
                for a in (0, 1):
                    for part in (0, 1):
                        fixed_low[state_rows(line, a, part), :] = fixed[line][a][part]
                        second[state_rows(line, a, part), :] = swept_high[line][a][part]
                        if own:
                            low[state_rows(line, a, part), :] = swept_low[line][a][part]


def times(ref, row, step, state):
    out = []
    for a in (0, 1):
        left, right = spread(ref, row + step * a, 8), spread(ref, row + step * a + 1, 8)
        out.append([left * x + right * y for x, y in zip(state[0], state[1])])
    return out


def response(ref, to, frm, state):
    if frm >= UNITS:
        to, frm = to - UNITS, frm - UNITS
    start, step = UNIT_START[to]
    return times(ref, VECTOR_ROWS + start + 2 * frm, step, state)


def total(first, *others):
    for other in others:
        first = [[p + q for p, q in zip(s, t)] for s, t in zip(first, other)]
    return first


def merge_kernel(bit, last, mine, other, edge, mids, *pair):
    is_low = jnp.bitwise_and(lax.axis_index("gy"), bit) == 0
    for low_side in (True, False):

        @pl.when(is_low if low_side else ~is_low)
        def _():
            lower, upper = (mine, other) if low_side else (other, mine)
            merge_records(bit, last, lower, upper, edge, mids, *pair)


def merge_records(bit, last, lower, upper, edge, mids, *pair):
    row = lax.broadcasted_iota(jnp.int32, (8, 128), 0)
    up = jnp.bitwise_and(row, 2) == 0

    def base(ref, chain, keep_up):
        wanted = (up if keep_up else ~up) & (row < unit_count(chain))
        out = []
        for a in (0, 1):
            units = ref[pl.ds(unit_row(chain, a), 8), :]
            out.append([ref[pl.ds(vector_row(chain, a), 8), :], jnp.where(wanted, units, 0.0)])
        return out

    low = functools.partial(response, lower)
    high = functools.partial(response, upper)
    m = [None] * 6
    m[T1] = base(lower, T1, True)
    m[U1] = total(base(upper, U1, False), high(U1, T1, m[T1]))
    m[T2] = total(base(lower, T2, True), low(T2, U1, m[U1]))
    m[U2] = total(base(upper, U2, False), high(U2, T1, m[T1]), high(U2, T2, m[T2]))
    m[T3] = total(base(lower, T3, True), low(T3, U1, m[U1]), low(T3, U2, m[U2]))
    m[U3] = total(base(upper, U3, False), high(U3, T1, m[T1]), high(U3, T2, m[T2]), high(U3, T3, m[T3]))
    e = [None] * 6
    for chain in range(6):
        ref, of = (upper, high) if CHAINS[chain][0] == 0 else (lower, low)
        through = [c for c in range(chain + 1) if CHAINS[c][0] == CHAINS[chain][0]]
        e[chain] = total(base(ref, chain, CHAINS[chain][0] == 1), *(of(chain, c, m[c]) for c in through))
    keep_record(mids, m)
    if not last:
        keep_record(edge, e)
        return
    next_low = jnp.bitwise_and(lax.axis_index("gy"), 2 * bit) == 0
    for chain in (T1, T2, T3):
        for a in (0, 1):
            place = pl.ds(vector_row(chain, a), 8)
            edge[place, :] = jnp.where(next_low, e[chain][a][0], e[chain + 1][a][0])
    for ref, table in zip(pair, (UP_ROWS, DOWN_ROWS)):
        ref[...] = jnp.zeros_like(ref)
        for (to, frm), (start, step) in table.items():
            for a in (0, 1):
                ref[pl.ds(start + step * a, 2), :] = e[to][a][1][2 * frm : 2 * frm + 2]
    units = pl.ds(VECTOR_ROWS // 2, LAST_UNITS)
    edge[units, :] = jnp.where(next_low, pair[0][...], pair[1][...])


def compose_kernel(lines, levels, *refs):
    mids, (fixed, second, early, late, own, away, first, low) = refs[: levels - 1], refs[levels - 1 :]
    place, core = lax.axis_index("gy"), lax.axis_index("gx")
    low[...] = jnp.where(core == 0, early[...], late[...])
    first[...] = low[...] + fixed[...]
    row = lax.broadcasted_iota(jnp.int32, (8, 128), 0)
    none = jnp.zeros((8, 128), jnp.float32)
    in_low = jnp.bitwise_and(place, 1 << (levels - 1)) == 0

    def select(condition, x, y):
        return [[jnp.where(condition, p, q) for p, q in zip(s, t)] for s, t in zip(x, y)]

    enters = []
    for direction, number in CHAINS:
        one = [jnp.where(row == 2 * number + a, 1.0, 0.0) for a in (0, 1)]
        here = in_low if direction else ~in_low
        enters.append([[none, jnp.where(here, one[a], 0.0)] for a in (0, 1)])
    for level in reversed(range(levels - 1)):
        ref = mids[level]
        m = []
        for chain in range(6):
            base = [[ref[pl.ds(vector_row(chain, a), 8), :], none] for a in (0, 1)]
            terms = [response(ref, chain, c, enters[c]) for c in feeds(chain)]
            if chain >= UNITS:
                terms += [response(ref, chain, c, enters[c]) for c in range(UNITS, chain + 1)]
            m.append(total(base, *terms))
        is_low = jnp.bitwise_and(place, 1 << level) == 0
        enters = [
            select(is_low, enters[c], m[c]) if CHAINS[c][0] == 0 else select(is_low, m[c], enters[c])
            for c in range(6)
        ]

    width = 8 + 2 * UNITS
    units = [(c, c) for c in range(UNITS)]
    for line in range(lines):
        for a in (0, 1):
            start = (2 * line + a) * width
            planes = []
            for source, extra in ((first, [(T1, T3), (U1, U3)]), (second, [])):
                value = [source[pl.ds(start, 8), :], none]
                pairs = [(source, start + 8, pair) for pair in units]
                pairs += [(low, start + 8, pair) for pair in extra]
                for ref, begin, (column, chain) in pairs:
                    for b in (0, 1):
                        factor = spread(ref, begin + 2 * column + b, 8)
                        value = [v + factor * e for v, e in zip(value, enters[chain][b])]
                planes.append(value)
            for part in (0, 1):
                mine, other = planes[0][part], planes[1][part]
                own[state_rows(line, a, part), :] = jnp.where(core == 0, mine, other)
                away[state_rows(line, a, part), :] = jnp.where(core == 0, other, mine)


def apply_map(lines, ref, entry, target):
    width = 8 + 2 * UNITS
    for line in range(lines):
        for a in (0, 1):
            start = (2 * line + a) * width
            value = ref[pl.ds(start, 8), :]
            for number in range(3):
                for b in (0, 1):
                    value = value + spread(ref, start + 8 + 2 * number + b, 8) * entry[number][b]
            target[pl.ds(line * 16 + a, 8, stride=2), :] = value


def finish_kernel(levels, mine, other, entry, ups, downs):
    is_low = jnp.bitwise_and(lax.axis_index("gy"), 1 << (levels - 1)) == 0
    x, y = mine[...], other[...]
    ups[...] = jnp.where(is_low, x, y)
    downs[...] = jnp.where(is_low, y, x)

    def base(ref, chain, first_chain):
        skip = vector_row(first_chain, 0)
        return [[ref[pl.ds(vector_row(chain, a) - skip, 8), :]] for a in (0, 1)]

    def up(to, frm, state):
        start, step = UP_ROWS[to, frm]
        return times(ups, VECTOR_ROWS // 2 + start, step, state)

    def down(to, frm, state):
        if frm >= UNITS:
            to, frm = to - UNITS, frm - UNITS
        start, step = DOWN_ROWS[to, frm]
        return times(downs, VECTOR_ROWS // 2 + start, step, state)

    m = [None] * 6
    m[T1] = base(ups, T1, T1)
    m[U1] = total(base(downs, U1, U1), down(U1, T1, m[T1]))
    m[T2] = total(base(ups, T2, T1), up(T2, U1, m[U1]))
    m[U2] = total(base(downs, U2, U1), down(U2, T1, m[T1]), down(U2, T2, m[T2]))
    m[T3] = total(base(ups, T3, T1), up(T3, U1, m[U1]), up(T3, U2, m[U2]))
    m[U3] = total(base(downs, U3, U1), down(U3, T1, m[T1]), down(U3, T2, m[T2]), down(U3, T3, m[T3]))
    enters = [
        [jnp.where(is_low, m[2 * number + 1][b][0], m[2 * number][b][0]) for b in (0, 1)] for number in range(3)
    ]
    for number in range(3):
        for b in (0, 1):
            entry[pl.ds((2 * number + b) * 8, 8), :] = enters[number][b]


def own_kernel(lines, entry, own, kept):
    enters = [[entry[pl.ds((2 * number + b) * 8, 8), :] for b in (0, 1)] for number in range(3)]
    apply_map(lines, own, enters, kept)


def part_copy(half, position, value, out, sem):
    lanes = pl.ds(pl.multiple_of(position * half, half), half)
    return pltpu.make_async_copy(value, out.at[0, :, :, :, lanes], sem)


def store_kernel(half, kept, out, sem):
    one = part_copy(half, half_of(), kept, out, sem.at[0])
    one.start()
    one.wait()


def last_kernel(half, got, before, out, sem):
    one = part_copy(half, 1 - half_of(), got, out, sem.at[0])
    one.start()
    one.wait()


def per_device(krylov, inverse, back, front, left, right):
    _, lines, vectors, _, cells = krylov.shape
    count = lax.axis_size("gy")
    levels = count.bit_length() - 1
    half = cells // 2
    width = vectors + 2 * UNITS
    assert lax.axis_size("gx") == 2 and count == 1 << levels and levels > 1
    assert vectors == 8 and half == 128
    swap = [(0, 1), (1, 0)]

    arguments = [pltpu.with_memory_space_constraint(x, pltpu.HBM) for x in (krylov, inverse, back, front, left, right)]

    def pack(away):
        (out,) = call(
            functools.partial(pack_kernel, half, vectors, away),
            [(lines, vectors + 8, 2, half)],
            arguments,
            [pltpu.SemaphoreType.DMA((5,))],
            specs=[HBM] * 6,
        )
        return out.reshape(-1, half)

    recv = lax.ppermute(pack(True), "gx", swap)
    keep = pack(False)
    swept, early, own_maps = call(
        functools.partial(early_kernel, lines, vectors),
        [(2 * lines * width, half), (ROWS, half), (12 * lines, half)],
        (keep,),
    )
    edge, fixed, second, late = call(
        functools.partial(local_kernel, lines, vectors),
        [(ROWS, half), (2 * lines * width, half), (2 * lines * width, half), (2 * lines * width, half)],
        (keep, recv, swept, early, own_maps),
        [pltpu.VMEM((12 * lines, half), jnp.float32)],
    )
    mids = []
    for level in range(levels - 1):
        got = lax.ppermute(edge, "gy", [(j, j ^ (1 << level)) for j in range(count)])
        last = level == levels - 2
        edge, mid = call(
            functools.partial(merge_kernel, 1 << level, last),
            [(LAST_ROWS if last else ROWS, half), (ROWS, half)],
            (edge, got),
            [pltpu.VMEM((LAST_UNITS, half), jnp.float32)] * (2 * last),
        )
        mids.append(mid)
    across = [(core * count + j, (1 - core) * count + (j ^ (count // 2))) for core in (0, 1) for j in range(count)]
    got = lax.ppermute(edge, ("gx", "gy"), across)
    own, away = call(
        functools.partial(compose_kernel, lines, levels),
        [(2 * lines * width, half)] * 2,
        (*mids, fixed, second, swept, late),
        [pltpu.VMEM((2 * lines * width, half), jnp.float32)] * 2,
    )
    away = lax.ppermute(away, "gx", swap)
    (entry,) = call(
        functools.partial(finish_kernel, levels),
        [(VECTOR_ROWS // 2, half)],
        (edge, got),
        [pltpu.VMEM((LAST_ROWS, half), jnp.float32)] * 2,
    )
    got_entry = lax.ppermute(entry, "gx", swap)

    def plane_half(carries, ref):
        (value,) = call(functools.partial(own_kernel, lines), [(lines * 16, half)], (carries, ref))
        return value.reshape(lines, vectors, 2, half)

    kept = plane_half(entry, own)
    (out,) = call(
        functools.partial(store_kernel, half),
        [krylov.shape],
        [kept],
        [pltpu.SemaphoreType.DMA((1,))],
        specs=[ANY],
        out_specs=[HBM],
    )
    (out,) = call(
        functools.partial(last_kernel, half),
        [krylov.shape],
        [plane_half(got_entry, away), out],
        [pltpu.SemaphoreType.DMA((1,))],
        specs=[ANY, HBM],
        out_specs=[HBM],
        aliases={1: 0},
    )
    return out


def solution(mesh):
    spec = P("gx", "gy", None, None, None)
    return jax.shard_map(
        per_device, mesh=mesh, in_specs=(spec,) * 6, out_specs=spec, check_vma=False
    )
```

```python
import functools

import jax
import jax.numpy as jnp
from jax import lax
from jax.experimental import pallas as pl
from jax.experimental.pallas import tpu as pltpu
from jax.sharding import PartitionSpec as P

CHAINS = ((0, 0), (1, 0), (0, 1), (1, 1), (0, 2), (1, 2))
T1, U1, T2, U2, T3, U3 = range(6)
UNITS = 4
VMEM = pl.BlockSpec(memory_space=pltpu.VMEM)
ANY = pl.BlockSpec(memory_space=pl.ANY)
HBM = pl.BlockSpec(memory_space=pltpu.HBM)


def spot(chain):
    direction, number = CHAINS[chain]
    return 3 * direction + number


def feeds(chain):
    return range(min(chain + 1, UNITS))


UNIT_START = {U1: (0, 4), T2: (8, 8), T1: (14, 8), U2: (24, 8), T3: (40, 8), U3: (56, 8)}
VECTOR_ROWS = 96
ROWS = VECTOR_ROWS + 72
UP_ROWS = {(T2, U1): (0, 2), (T3, U1): (4, 4), (T3, U2): (6, 4)}
DOWN_ROWS = {(U1, T1): (0, 2), (U2, T1): (4, 4), (U2, T2): (6, 4), (U3, T1): (12, 4), (U3, T2): (14, 4)}
LAST_UNITS = 24
LAST_ROWS = VECTOR_ROWS // 2 + LAST_UNITS


def vector_row(chain, a):
    return (2 * spot(chain) + a) * 8


def unit_row(chain, a):
    start, step = UNIT_START[chain]
    return VECTOR_ROWS + start + step * a


def unit_count(chain):
    return 2 * len(feeds(chain))


def half_of():
    top = lax.axis_size("gy") // 2
    flip = jnp.where(jnp.bitwise_and(lax.axis_index("gy"), top) == 0, 0, 1)
    return jnp.bitwise_xor(lax.axis_index("gx"), flip)


def keep_record(ref, values, chains=range(6)):
    for chain in chains:
        for a in (0, 1):
            carries, units = values[chain][a]
            ref[pl.ds(vector_row(chain, a), 8), :] = carries
            count = unit_count(chain)
            ref[pl.ds(unit_row(chain, a), count), :] = units[:count]


def spread(ref, row, count):
    return ref[pl.ds(row, count, stride=0), :]


def call(kernel, outs, ins, scratch=(), specs=None, out_specs=None, aliases={}):
    return pl.pallas_call(
        kernel,
        out_shape=[jax.ShapeDtypeStruct(s, jnp.float32) for s in outs],
        in_specs=specs or [VMEM] * len(ins),
        out_specs=out_specs or [VMEM] * len(outs),
        scratch_shapes=list(scratch),
        input_output_aliases=aliases,
        compiler_params=pltpu.CompilerParams(vmem_limit_bytes=8 << 20),
    )(*ins)


def pack_kernel(half, vectors, away, krylov, inverse, back, front, left, right, out, sems):
    core, part = lax.axis_index("gx"), half_of()
    position = 1 - part if away else part
    lanes = pl.ds(pl.multiple_of(position * half, half), half)
    base = (0, vectors, vectors + 2, vectors + 4, vectors + 6)

    def copy(ref, number):
        target = out.at[:, pl.ds(base[number], ref.shape[2])]
        return pltpu.make_async_copy(ref.at[0, :, :, :, lanes], target, sems.at[number])

    plan = [copy(ref, number) for number, ref in enumerate((krylov, inverse, left, right))]
    for one in plan:
        one.start()
    for own, ref in ((0, front), (1, back)):

        @pl.when(core == own)
        def _():
            one = copy(ref, 4)
            one.start()
            one.wait()

    for one in plan:
        one.wait()


def combine(ref, place, state):
    out = []
    for a in (0, 1):
        left, right = (spread(ref, place(a, b), 8) for b in (0, 1))
        out.append([left * x + right * y for x, y in zip(state[0], state[1])])
    return out


def add(x, y):
    return [[p + q for p, q in zip(s, t)] + t[len(s) :] for s, t in zip(x, y)]


FORWARD, BACKWARD, ACROSS = range(3)


def make_maps(lines, vectors, data, maps):
    pitch = 2 * vectors + 16

    def block(number):
        start = 2 * vectors + 4 * number
        return [[data[pl.ds(start + 2 * a + b, lines, stride=pitch), :] for b in (0, 1)] for a in (0, 1)]

    inverse = block(0)
    for number in (FORWARD, BACKWARD, ACROSS):
        coupling = block(1 + number)
        for a in (0, 1):
            for b in (0, 1):
                value = -(inverse[a][0] * coupling[0][b] + inverse[a][1] * coupling[1][b])
                maps[pl.ds((4 * number + 2 * a + b) * lines, lines), :] = value


def mapped(lines, maps, number, line, state):
    return combine(maps, lambda a, b: (4 * number + 2 * a + b) * lines + line, state)


def scaled(vectors, data, line):
    start = line * (2 * vectors + 16)
    source = [[data[pl.ds(start + a, vectors, stride=2), :]] for a in (0, 1)]
    return combine(data, lambda a, b: start + 2 * vectors + 2 * a + b, source)


def unit(chain):
    row = lax.broadcasted_iota(jnp.int32, (8, 128), 0)
    none = jnp.zeros((8, 128), jnp.float32)
    one = [jnp.where(row == 2 * chain + a, 1.0, 0.0) if chain < UNITS else none for a in (0, 1)]
    return [[none, one[a]] for a in (0, 1)]


def sweep_plane(lines, maps, chain, source, leaving):
    state, states = unit(chain), []
    for line in range(lines):
        first = line == 0 and chain >= UNITS
        state = source(line) if first else add(source(line), mapped(lines, maps, FORWARD, line, state))
        states.append(state)
    leaving[chain] = state
    state, result = unit(chain + 1), [None] * lines
    for line in reversed(range(lines)):
        first = line == lines - 1 and chain + 1 >= UNITS
        state = states[line] if first else add(states[line], mapped(lines, maps, BACKWARD, line, state))
        result[line] = state
    leaving[chain + 1] = state
    return result


def state_rows(line, a, part):
    return pl.ds((2 * line + a) * (8 + 2 * UNITS) + 8 * part, 8)


def early_kernel(lines, vectors, keep, swept, edge, maps):
    make_maps(lines, vectors, keep, maps)

    @pl.when(lax.axis_index("gx") == 0)
    def _():
        leaving = [None] * 6
        result = sweep_plane(lines, maps, T1, lambda line: scaled(vectors, keep, line), leaving)
        keep_record(edge, leaving, (T1, U1))
        for line in range(lines):
            for a in (0, 1):
                for part in (0, 1):
                    swept[state_rows(line, a, part), :] = result[line][a][part]


def local_kernel(lines, vectors, keep, recv, swept, early, own_maps, edge, first, second, low, other_maps):
    make_maps(lines, vectors, recv, other_maps)
    for own in (0, 1):

        @pl.when(lax.axis_index("gx") == own)
        def _():
            leaving = [None] * 6
            maps = (other_maps, own_maps) if own else (own_maps, other_maps)
            if own == 0:
                swept_low = [
                    [[swept[state_rows(line, a, part), :] for part in (0, 1)] for a in (0, 1)] for line in range(lines)
                ]
                for chain in (T1, U1):
                    leaving[chain] = [
                        [early[pl.ds(vector_row(chain, a), 8), :], early[pl.ds(unit_row(chain, a), 8), :]] for a in (0, 1)
                    ]
            else:
                swept_low = sweep_plane(lines, maps[0], T1, lambda line: scaled(vectors, recv, line), leaving)
            high_data = keep if own else recv
            swept_high = sweep_plane(
                lines,
                maps[1],
                T2,
                lambda line: add(scaled(vectors, high_data, line), mapped(lines, maps[1], ACROSS, line, swept_low[line])),
                leaving,
            )
            fixed = sweep_plane(
                lines, maps[0], T3, lambda line: mapped(lines, maps[0], ACROSS, line, swept_high[line]), leaving
            )
            keep_record(edge, leaving)
            for line in range(lines):
                total = add(swept_low[line], fixed[line])
                for a in (0, 1):
                    low[pl.ds((2 * line + a) * 8, 8), :] = swept_low[line][a][1]
                    for part in (0, 1):
                        first[state_rows(line, a, part), :] = total[a][part]
                        second[state_rows(line, a, part), :] = swept_high[line][a][part]


def times(ref, row, step, state):
    out = []
    for a in (0, 1):
        left, right = spread(ref, row + step * a, 8), spread(ref, row + step * a + 1, 8)
        out.append([left * x + right * y for x, y in zip(state[0], state[1])])
    return out


def response(ref, to, frm, state):
    if frm >= UNITS:
        to, frm = to - UNITS, frm - UNITS
    start, step = UNIT_START[to]
    return times(ref, VECTOR_ROWS + start + 2 * frm, step, state)


def total(first, *others):
    for other in others:
        first = [[p + q for p, q in zip(s, t)] for s, t in zip(first, other)]
    return first


def merge_kernel(bit, last, mine, other, edge, mids, *pair):
    is_low = jnp.bitwise_and(lax.axis_index("gy"), bit) == 0
    for low_side in (True, False):

        @pl.when(is_low if low_side else ~is_low)
        def _():
            lower, upper = (mine, other) if low_side else (other, mine)
            merge_records(bit, last, lower, upper, edge, mids, *pair)


def merge_records(bit, last, lower, upper, edge, mids, *pair):
    row = lax.broadcasted_iota(jnp.int32, (8, 128), 0)
    up = jnp.bitwise_and(row, 2) == 0

    def base(ref, chain, keep_up):
        wanted = (up if keep_up else ~up) & (row < unit_count(chain))
        out = []
        for a in (0, 1):
            units = ref[pl.ds(unit_row(chain, a), 8), :]
            out.append([ref[pl.ds(vector_row(chain, a), 8), :], jnp.where(wanted, units, 0.0)])
        return out

    low = functools.partial(response, lower)
    high = functools.partial(response, upper)
    m = [None] * 6
    m[T1] = base(lower, T1, True)
    m[U1] = total(base(upper, U1, False), high(U1, T1, m[T1]))
    m[T2] = total(base(lower, T2, True), low(T2, U1, m[U1]))
    m[U2] = total(base(upper, U2, False), high(U2, T1, m[T1]), high(U2, T2, m[T2]))
    m[T3] = total(base(lower, T3, True), low(T3, U1, m[U1]), low(T3, U2, m[U2]))
    m[U3] = total(base(upper, U3, False), high(U3, T1, m[T1]), high(U3, T2, m[T2]), high(U3, T3, m[T3]))
    e = [None] * 6
    for chain in range(6):
        ref, of = (upper, high) if CHAINS[chain][0] == 0 else (lower, low)
        through = [c for c in range(chain + 1) if CHAINS[c][0] == CHAINS[chain][0]]
        e[chain] = total(base(ref, chain, CHAINS[chain][0] == 1), *(of(chain, c, m[c]) for c in through))
    keep_record(mids, m)
    if not last:
        keep_record(edge, e)
        return
    next_low = jnp.bitwise_and(lax.axis_index("gy"), 2 * bit) == 0
    for chain in (T1, T2, T3):
        for a in (0, 1):
            place = pl.ds(vector_row(chain, a), 8)
            edge[place, :] = jnp.where(next_low, e[chain][a][0], e[chain + 1][a][0])
    for ref, table in zip(pair, (UP_ROWS, DOWN_ROWS)):
        ref[...] = jnp.zeros_like(ref)
        for (to, frm), (start, step) in table.items():
            for a in (0, 1):
                ref[pl.ds(start + step * a, 2), :] = e[to][a][1][2 * frm : 2 * frm + 2]
    units = pl.ds(VECTOR_ROWS // 2, LAST_UNITS)
    edge[units, :] = jnp.where(next_low, pair[0][...], pair[1][...])


def compose_kernel(lines, levels, *refs):
    mids, (first, second, low, own, away) = refs[: levels - 1], refs[levels - 1 :]
    place, core = lax.axis_index("gy"), lax.axis_index("gx")
    row = lax.broadcasted_iota(jnp.int32, (8, 128), 0)
    none = jnp.zeros((8, 128), jnp.float32)
    in_low = jnp.bitwise_and(place, 1 << (levels - 1)) == 0

    def select(condition, x, y):
        return [[jnp.where(condition, p, q) for p, q in zip(s, t)] for s, t in zip(x, y)]

    enters = []
    for direction, number in CHAINS:
        one = [jnp.where(row == 2 * number + a, 1.0, 0.0) for a in (0, 1)]
        here = in_low if direction else ~in_low
        enters.append([[none, jnp.where(here, one[a], 0.0)] for a in (0, 1)])
    for level in reversed(range(levels - 1)):
        ref = mids[level]
        m = []
        for chain in range(6):
            base = [[ref[pl.ds(vector_row(chain, a), 8), :], none] for a in (0, 1)]
            terms = [response(ref, chain, c, enters[c]) for c in feeds(chain)]
            if chain >= UNITS:
                terms += [response(ref, chain, c, enters[c]) for c in range(UNITS, chain + 1)]
            m.append(total(base, *terms))
        is_low = jnp.bitwise_and(place, 1 << level) == 0
        enters = [
            select(is_low, enters[c], m[c]) if CHAINS[c][0] == 0 else select(is_low, m[c], enters[c])
            for c in range(6)
        ]

    width = 8 + 2 * UNITS
    units = [(c, c) for c in range(UNITS)]
    for line in range(lines):
        for a in (0, 1):
            start = (2 * line + a) * width
            planes = []
            for source, extra in ((first, [(T1, T3), (U1, U3)]), (second, [])):
                value = [source[pl.ds(start, 8), :], none]
                pairs = [(source, start + 8, pair) for pair in units]
                pairs += [(low, (2 * line + a) * 8, pair) for pair in extra]
                for ref, begin, (column, chain) in pairs:
                    for b in (0, 1):
                        factor = spread(ref, begin + 2 * column + b, 8)
                        value = [v + factor * e for v, e in zip(value, enters[chain][b])]
                planes.append(value)
            for part in (0, 1):
                mine, other = planes[0][part], planes[1][part]
                own[state_rows(line, a, part), :] = jnp.where(core == 0, mine, other)
                away[state_rows(line, a, part), :] = jnp.where(core == 0, other, mine)


def apply_map(lines, ref, entry, target):
    width = 8 + 2 * UNITS
    for line in range(lines):
        for a in (0, 1):
            start = (2 * line + a) * width
            value = ref[pl.ds(start, 8), :]
            for number in range(3):
                for b in (0, 1):
                    value = value + spread(ref, start + 8 + 2 * number + b, 8) * entry[number][b]
            target[pl.ds(line * 16 + a, 8, stride=2), :] = value


def finish_kernel(levels, mine, other, entry, ups, downs):
    is_low = jnp.bitwise_and(lax.axis_index("gy"), 1 << (levels - 1)) == 0
    x, y = mine[...], other[...]
    ups[...] = jnp.where(is_low, x, y)
    downs[...] = jnp.where(is_low, y, x)

    def base(ref, chain, first_chain):
        skip = vector_row(first_chain, 0)
        return [[ref[pl.ds(vector_row(chain, a) - skip, 8), :]] for a in (0, 1)]

    def up(to, frm, state):
        start, step = UP_ROWS[to, frm]
        return times(ups, VECTOR_ROWS // 2 + start, step, state)

    def down(to, frm, state):
        if frm >= UNITS:
            to, frm = to - UNITS, frm - UNITS
        start, step = DOWN_ROWS[to, frm]
        return times(downs, VECTOR_ROWS // 2 + start, step, state)

    m = [None] * 6
    m[T1] = base(ups, T1, T1)
    m[U1] = total(base(downs, U1, U1), down(U1, T1, m[T1]))
    m[T2] = total(base(ups, T2, T1), up(T2, U1, m[U1]))
    m[U2] = total(base(downs, U2, U1), down(U2, T1, m[T1]), down(U2, T2, m[T2]))
    m[T3] = total(base(ups, T3, T1), up(T3, U1, m[U1]), up(T3, U2, m[U2]))
    m[U3] = total(base(downs, U3, U1), down(U3, T1, m[T1]), down(U3, T2, m[T2]), down(U3, T3, m[T3]))
    enters = [
        [jnp.where(is_low, m[2 * number + 1][b][0], m[2 * number][b][0]) for b in (0, 1)] for number in range(3)
    ]
    for number in range(3):
        for b in (0, 1):
            entry[pl.ds((2 * number + b) * 8, 8), :] = enters[number][b]


def own_kernel(lines, entry, own, kept):
    enters = [[entry[pl.ds((2 * number + b) * 8, 8), :] for b in (0, 1)] for number in range(3)]
    apply_map(lines, own, enters, kept)


def part_copy(half, position, value, out, sem):
    lanes = pl.ds(pl.multiple_of(position * half, half), half)
    return pltpu.make_async_copy(value, out.at[0, :, :, :, lanes], sem)


def store_kernel(half, kept, out, sem):
    one = part_copy(half, half_of(), kept, out, sem.at[0])
    one.start()
    one.wait()


def last_kernel(lines, half, entry, away, before, out, value, sem):
    own_kernel(lines, entry, away, value)
    one = part_copy(half, 1 - half_of(), value.reshape(lines, value.shape[0] // (2 * lines), 2, half), out, sem.at[0])
    one.start()
    one.wait()


def per_device(krylov, inverse, back, front, left, right):
    _, lines, vectors, _, cells = krylov.shape
    count = lax.axis_size("gy")
    levels = count.bit_length() - 1
    half = cells // 2
    width = vectors + 2 * UNITS
    assert lax.axis_size("gx") == 2 and count == 1 << levels and levels > 1
    assert vectors == 8 and half == 128
    swap = [(0, 1), (1, 0)]

    arguments = [pltpu.with_memory_space_constraint(x, pltpu.HBM) for x in (krylov, inverse, back, front, left, right)]

    def pack(away):
        (out,) = call(
            functools.partial(pack_kernel, half, vectors, away),
            [(lines, vectors + 8, 2, half)],
            arguments,
            [pltpu.SemaphoreType.DMA((5,))],
            specs=[HBM] * 6,
        )
        return out.reshape(-1, half)

    recv = lax.ppermute(pack(True), "gx", swap)
    keep = pack(False)
    swept, early, own_maps = call(
        functools.partial(early_kernel, lines, vectors),
        [(2 * lines * width, half), (ROWS, half), (12 * lines, half)],
        (keep,),
    )
    edge, first, second, low = call(
        functools.partial(local_kernel, lines, vectors),
        [(ROWS, half), (2 * lines * width, half), (2 * lines * width, half), (2 * lines * 8, half)],
        (keep, recv, swept, early, own_maps),
        [pltpu.VMEM((12 * lines, half), jnp.float32)],
    )
    mids = []
    for level in range(levels - 1):
        got = lax.ppermute(edge, "gy", [(j, j ^ (1 << level)) for j in range(count)])
        last = level == levels - 2
        edge, mid = call(
            functools.partial(merge_kernel, 1 << level, last),
            [(LAST_ROWS if last else ROWS, half), (ROWS, half)],
            (edge, got),
            [pltpu.VMEM((LAST_UNITS, half), jnp.float32)] * (2 * last),
        )
        mids.append(mid)
    across = [(core * count + j, (1 - core) * count + (j ^ (count // 2))) for core in (0, 1) for j in range(count)]
    got = lax.ppermute(edge, ("gx", "gy"), across)
    own, away = call(
        functools.partial(compose_kernel, lines, levels), [(2 * lines * width, half)] * 2, (*mids, first, second, low)
    )
    away = lax.ppermute(away, "gx", swap)
    (entry,) = call(
        functools.partial(finish_kernel, levels),
        [(VECTOR_ROWS // 2, half)],
        (edge, got),
        [pltpu.VMEM((LAST_ROWS, half), jnp.float32)] * 2,
    )
    got_entry = lax.ppermute(entry, "gx", swap)

    def plane_half(carries, ref):
        (value,) = call(functools.partial(own_kernel, lines), [(lines * 16, half)], (carries, ref))
        return value.reshape(lines, vectors, 2, half)

    kept = plane_half(entry, own)
    (out,) = call(
        functools.partial(store_kernel, half),
        [krylov.shape],
        [kept],
        [pltpu.SemaphoreType.DMA((1,))],
        specs=[ANY],
        out_specs=[HBM],
    )
    (out,) = call(
        functools.partial(last_kernel, lines, half),
        [krylov.shape],
        [got_entry, away, out],
        [pltpu.VMEM((lines * 16, half), jnp.float32), pltpu.SemaphoreType.DMA((1,))],
        specs=[VMEM, VMEM, HBM],
        out_specs=[HBM],
        aliases={2: 0},
    )
    return out


def solution(mesh):
    spec = P("gx", "gy", None, None, None)
    return jax.shard_map(
        per_device, mesh=mesh, in_specs=(spec,) * 6, out_specs=spec, check_vma=False
    )
```

```python
import functools

import jax
import jax.numpy as jnp
from jax import lax
from jax.experimental import pallas as pl
from jax.experimental.pallas import tpu as pltpu
from jax.sharding import PartitionSpec as P

CHAINS = ((0, 0), (1, 0), (0, 1), (1, 1), (0, 2), (1, 2))
T1, U1, T2, U2, T3, U3 = range(6)
UNITS = 4
VMEM = pl.BlockSpec(memory_space=pltpu.VMEM)
ANY = pl.BlockSpec(memory_space=pl.ANY)
HBM = pl.BlockSpec(memory_space=pltpu.HBM)


def spot(chain):
    direction, number = CHAINS[chain]
    return 3 * direction + number


def feeds(chain):
    return range(min(chain + 1, UNITS))


UNIT_START = {U1: (0, 4), T2: (8, 8), T1: (14, 8), U2: (24, 8), T3: (40, 8), U3: (56, 8)}
VECTOR_ROWS = 96
ROWS = VECTOR_ROWS + 72
UP_ROWS = {(T2, U1): (0, 2), (T3, U1): (4, 4), (T3, U2): (6, 4)}
DOWN_ROWS = {(U1, T1): (0, 2), (U2, T1): (4, 4), (U2, T2): (6, 4), (U3, T1): (12, 4), (U3, T2): (14, 4)}
LAST_UNITS = 24
LAST_ROWS = VECTOR_ROWS // 2 + LAST_UNITS


def vector_row(chain, a):
    return (2 * spot(chain) + a) * 8


def unit_row(chain, a):
    start, step = UNIT_START[chain]
    return VECTOR_ROWS + start + step * a


def unit_count(chain):
    return 2 * len(feeds(chain))


def half_of():
    top = lax.axis_size("gy") // 2
    flip = jnp.where(jnp.bitwise_and(lax.axis_index("gy"), top) == 0, 0, 1)
    return jnp.bitwise_xor(lax.axis_index("gx"), flip)


def keep_record(ref, values, chains=range(6)):
    for chain in chains:
        for a in (0, 1):
            carries, units = values[chain][a]
            ref[pl.ds(vector_row(chain, a), 8), :] = carries
            count = unit_count(chain)
            ref[pl.ds(unit_row(chain, a), count), :] = units[:count]


def spread(ref, row, count):
    return ref[pl.ds(row, count, stride=0), :]


def call(kernel, outs, ins, scratch=(), specs=None, out_specs=None, aliases={}):
    return pl.pallas_call(
        kernel,
        out_shape=[jax.ShapeDtypeStruct(s, jnp.float32) for s in outs],
        in_specs=specs or [VMEM] * len(ins),
        out_specs=out_specs or [VMEM] * len(outs),
        scratch_shapes=list(scratch),
        input_output_aliases=aliases,
        compiler_params=pltpu.CompilerParams(vmem_limit_bytes=8 << 20),
    )(*ins)


def pack_kernel(half, vectors, away, krylov, inverse, back, front, left, right, out, sems):
    core, part = lax.axis_index("gx"), half_of()
    position = 1 - part if away else part
    lanes = pl.ds(pl.multiple_of(position * half, half), half)
    base = (0, vectors, vectors + 2, vectors + 4, vectors + 6)

    def copy(ref, number):
        target = out.at[:, pl.ds(base[number], ref.shape[2])]
        return pltpu.make_async_copy(ref.at[0, :, :, :, lanes], target, sems.at[number])

    plan = [copy(ref, number) for number, ref in enumerate((krylov, inverse, left, right))]
    for one in plan:
        one.start()
    for own, ref in ((0, front), (1, back)):

        @pl.when(core == own)
        def _():
            one = copy(ref, 4)
            one.start()
            one.wait()

    for one in plan:
        one.wait()


def combine(ref, place, state):
    out = []
    for a in (0, 1):
        left, right = (spread(ref, place(a, b), 8) for b in (0, 1))
        out.append([left * x + right * y for x, y in zip(state[0], state[1])])
    return out


def add(x, y):
    return [[p + q for p, q in zip(s, t)] + t[len(s) :] for s, t in zip(x, y)]


FORWARD, BACKWARD, ACROSS = range(3)


def make_maps(lines, vectors, data, maps):
    pitch = 2 * vectors + 16

    def block(number):
        start = 2 * vectors + 4 * number
        return [[data[pl.ds(start + 2 * a + b, lines, stride=pitch), :] for b in (0, 1)] for a in (0, 1)]

    inverse = block(0)
    for number in (FORWARD, BACKWARD, ACROSS):
        coupling = block(1 + number)
        for a in (0, 1):
            for b in (0, 1):
                value = -(inverse[a][0] * coupling[0][b] + inverse[a][1] * coupling[1][b])
                maps[pl.ds((4 * number + 2 * a + b) * lines, lines), :] = value


def mapped(lines, maps, number, line, state):
    return combine(maps, lambda a, b: (4 * number + 2 * a + b) * lines + line, state)


def scaled(vectors, data, line):
    start = line * (2 * vectors + 16)
    source = [[data[pl.ds(start + a, vectors, stride=2), :]] for a in (0, 1)]
    return combine(data, lambda a, b: start + 2 * vectors + 2 * a + b, source)


def unit(chain):
    row = lax.broadcasted_iota(jnp.int32, (8, 128), 0)
    none = jnp.zeros((8, 128), jnp.float32)
    one = [jnp.where(row == 2 * chain + a, 1.0, 0.0) if chain < UNITS else none for a in (0, 1)]
    return [[none, one[a]] for a in (0, 1)]


def sweep_plane(lines, maps, chain, source, leaving):
    state, states = unit(chain), []
    for line in range(lines):
        first = line == 0 and chain >= UNITS
        state = source(line) if first else add(source(line), mapped(lines, maps, FORWARD, line, state))
        states.append(state)
    leaving[chain] = state
    state, result = unit(chain + 1), [None] * lines
    for line in reversed(range(lines)):
        first = line == lines - 1 and chain + 1 >= UNITS
        state = states[line] if first else add(states[line], mapped(lines, maps, BACKWARD, line, state))
        result[line] = state
    leaving[chain + 1] = state
    return result


def state_rows(line, a, part):
    return pl.ds((2 * line + a) * (8 + 2 * UNITS) + 8 * part, 8)


def early_kernel(lines, vectors, keep, swept, edge, maps):
    make_maps(lines, vectors, keep, maps)

    @pl.when(lax.axis_index("gx") == 0)
    def _():
        leaving = [None] * 6
        result = sweep_plane(lines, maps, T1, lambda line: scaled(vectors, keep, line), leaving)
        keep_record(edge, leaving, (T1, U1))
        for line in range(lines):
            for a in (0, 1):
                for part in (0, 1):
                    swept[state_rows(line, a, part), :] = result[line][a][part]


def local_kernel(lines, vectors, keep, recv, swept, early, own_maps, edge, fixed_low, second, low, other_maps):
    make_maps(lines, vectors, recv, other_maps)
    for own in (0, 1):

        @pl.when(lax.axis_index("gx") == own)
        def _():
            leaving = [None] * 6
            maps = (other_maps, own_maps) if own else (own_maps, other_maps)
            if own == 0:
                swept_low = [
                    [[swept[state_rows(line, a, part), :] for part in (0, 1)] for a in (0, 1)] for line in range(lines)
                ]
                for chain in (T1, U1):
                    leaving[chain] = [
                        [early[pl.ds(vector_row(chain, a), 8), :], early[pl.ds(unit_row(chain, a), 8), :]] for a in (0, 1)
                    ]
            else:
                swept_low = sweep_plane(lines, maps[0], T1, lambda line: scaled(vectors, recv, line), leaving)
            high_data = keep if own else recv
            swept_high = sweep_plane(
                lines,
                maps[1],
                T2,
                lambda line: add(scaled(vectors, high_data, line), mapped(lines, maps[1], ACROSS, line, swept_low[line])),
                leaving,
            )
            fixed = sweep_plane(
                lines, maps[0], T3, lambda line: mapped(lines, maps[0], ACROSS, line, swept_high[line]), leaving
            )
            keep_record(edge, leaving)
            for line in range(lines):
                for a in (0, 1):
                    for part in (0, 1):
                        fixed_low[state_rows(line, a, part), :] = fixed[line][a][part]
                        second[state_rows(line, a, part), :] = swept_high[line][a][part]
                        if own:
                            low[state_rows(line, a, part), :] = swept_low[line][a][part]


def times(ref, row, step, state):
    out = []
    for a in (0, 1):
        left, right = spread(ref, row + step * a, 8), spread(ref, row + step * a + 1, 8)
        out.append([left * x + right * y for x, y in zip(state[0], state[1])])
    return out


def response(ref, to, frm, state):
    if frm >= UNITS:
        to, frm = to - UNITS, frm - UNITS
    start, step = UNIT_START[to]
    return times(ref, VECTOR_ROWS + start + 2 * frm, step, state)


def total(first, *others):
    for other in others:
        first = [[p + q for p, q in zip(s, t)] for s, t in zip(first, other)]
    return first


def merge_kernel(bit, last, mine, other, edge, mids, *pair):
    is_low = jnp.bitwise_and(lax.axis_index("gy"), bit) == 0
    for low_side in (True, False):

        @pl.when(is_low if low_side else ~is_low)
        def _():
            lower, upper = (mine, other) if low_side else (other, mine)
            merge_records(bit, last, lower, upper, edge, mids, *pair)


def merge_records(bit, last, lower, upper, edge, mids, *pair):
    row = lax.broadcasted_iota(jnp.int32, (8, 128), 0)
    up = jnp.bitwise_and(row, 2) == 0

    def base(ref, chain, keep_up):
        wanted = (up if keep_up else ~up) & (row < unit_count(chain))
        out = []
        for a in (0, 1):
            units = ref[pl.ds(unit_row(chain, a), 8), :]
            out.append([ref[pl.ds(vector_row(chain, a), 8), :], jnp.where(wanted, units, 0.0)])
        return out

    low = functools.partial(response, lower)
    high = functools.partial(response, upper)
    m = [None] * 6
    m[T1] = base(lower, T1, True)
    m[U1] = total(base(upper, U1, False), high(U1, T1, m[T1]))
    m[T2] = total(base(lower, T2, True), low(T2, U1, m[U1]))
    m[U2] = total(base(upper, U2, False), high(U2, T1, m[T1]), high(U2, T2, m[T2]))
    m[T3] = total(base(lower, T3, True), low(T3, U1, m[U1]), low(T3, U2, m[U2]))
    m[U3] = total(base(upper, U3, False), high(U3, T1, m[T1]), high(U3, T2, m[T2]), high(U3, T3, m[T3]))
    e = [None] * 6
    for chain in range(6):
        ref, of = (upper, high) if CHAINS[chain][0] == 0 else (lower, low)
        through = [c for c in range(chain + 1) if CHAINS[c][0] == CHAINS[chain][0]]
        e[chain] = total(base(ref, chain, CHAINS[chain][0] == 1), *(of(chain, c, m[c]) for c in through))
    keep_record(mids, m)
    if not last:
        keep_record(edge, e)
        return
    next_low = jnp.bitwise_and(lax.axis_index("gy"), 2 * bit) == 0
    for chain in (T1, T2, T3):
        for a in (0, 1):
            place = pl.ds(vector_row(chain, a), 8)
            edge[place, :] = jnp.where(next_low, e[chain][a][0], e[chain + 1][a][0])
    for ref, table in zip(pair, (UP_ROWS, DOWN_ROWS)):
        ref[...] = jnp.zeros_like(ref)
        for (to, frm), (start, step) in table.items():
            for a in (0, 1):
                ref[pl.ds(start + step * a, 2), :] = e[to][a][1][2 * frm : 2 * frm + 2]
    units = pl.ds(VECTOR_ROWS // 2, LAST_UNITS)
    edge[units, :] = jnp.where(next_low, pair[0][...], pair[1][...])


def compose_kernel(lines, levels, *refs):
    mids, (fixed, second, early, late, own, away, first, low) = refs[: levels - 1], refs[levels - 1 :]
    place, core = lax.axis_index("gy"), lax.axis_index("gx")
    low[...] = jnp.where(core == 0, early[...], late[...])
    first[...] = low[...] + fixed[...]
    row = lax.broadcasted_iota(jnp.int32, (8, 128), 0)
    none = jnp.zeros((8, 128), jnp.float32)
    in_low = jnp.bitwise_and(place, 1 << (levels - 1)) == 0

    def select(condition, x, y):
        return [[jnp.where(condition, p, q) for p, q in zip(s, t)] for s, t in zip(x, y)]

    enters = []
    for direction, number in CHAINS:
        one = [jnp.where(row == 2 * number + a, 1.0, 0.0) for a in (0, 1)]
        here = in_low if direction else ~in_low
        enters.append([[none, jnp.where(here, one[a], 0.0)] for a in (0, 1)])
    for level in reversed(range(levels - 1)):
        ref = mids[level]
        m = []
        for chain in range(6):
            base = [[ref[pl.ds(vector_row(chain, a), 8), :], none] for a in (0, 1)]
            terms = [response(ref, chain, c, enters[c]) for c in feeds(chain)]
            if chain >= UNITS:
                terms += [response(ref, chain, c, enters[c]) for c in range(UNITS, chain + 1)]
            m.append(total(base, *terms))
        is_low = jnp.bitwise_and(place, 1 << level) == 0
        enters = [
            select(is_low, enters[c], m[c]) if CHAINS[c][0] == 0 else select(is_low, m[c], enters[c])
            for c in range(6)
        ]

    width = 8 + 2 * UNITS
    units = [(c, c) for c in range(UNITS)]
    for line in range(lines):
        for a in (0, 1):
            start = (2 * line + a) * width
            planes = []
            for source, extra in ((first, [(T1, T3), (U1, U3)]), (second, [])):
                value = [source[pl.ds(start, 8), :], none]
                pairs = [(source, start + 8, pair) for pair in units]
                pairs += [(low, start + 8, pair) for pair in extra]
                for ref, begin, (column, chain) in pairs:
                    for b in (0, 1):
                        factor = spread(ref, begin + 2 * column + b, 8)
                        value = [v + factor * e for v, e in zip(value, enters[chain][b])]
                planes.append(value)
            for part in (0, 1):
                mine, other = planes[0][part], planes[1][part]
                own[state_rows(line, a, part), :] = jnp.where(core == 0, mine, other)
                away[state_rows(line, a, part), :] = jnp.where(core == 0, other, mine)


def apply_map(lines, ref, entry, target):
    width = 8 + 2 * UNITS
    for line in range(lines):
        for a in (0, 1):
            start = (2 * line + a) * width
            value = ref[pl.ds(start, 8), :]
            for number in range(3):
                for b in (0, 1):
                    value = value + spread(ref, start + 8 + 2 * number + b, 8) * entry[number][b]
            target[pl.ds(line * 16 + a, 8, stride=2), :] = value


def finish_kernel(levels, mine, other, entry, ups, downs):
    is_low = jnp.bitwise_and(lax.axis_index("gy"), 1 << (levels - 1)) == 0
    x, y = mine[...], other[...]
    ups[...] = jnp.where(is_low, x, y)
    downs[...] = jnp.where(is_low, y, x)

    def base(ref, chain, first_chain):
        skip = vector_row(first_chain, 0)
        return [[ref[pl.ds(vector_row(chain, a) - skip, 8), :]] for a in (0, 1)]

    def up(to, frm, state):
        start, step = UP_ROWS[to, frm]
        return times(ups, VECTOR_ROWS // 2 + start, step, state)

    def down(to, frm, state):
        if frm >= UNITS:
            to, frm = to - UNITS, frm - UNITS
        start, step = DOWN_ROWS[to, frm]
        return times(downs, VECTOR_ROWS // 2 + start, step, state)

    m = [None] * 6
    m[T1] = base(ups, T1, T1)
    m[U1] = total(base(downs, U1, U1), down(U1, T1, m[T1]))
    m[T2] = total(base(ups, T2, T1), up(T2, U1, m[U1]))
    m[U2] = total(base(downs, U2, U1), down(U2, T1, m[T1]), down(U2, T2, m[T2]))
    m[T3] = total(base(ups, T3, T1), up(T3, U1, m[U1]), up(T3, U2, m[U2]))
    m[U3] = total(base(downs, U3, U1), down(U3, T1, m[T1]), down(U3, T2, m[T2]), down(U3, T3, m[T3]))
    enters = [
        [jnp.where(is_low, m[2 * number + 1][b][0], m[2 * number][b][0]) for b in (0, 1)] for number in range(3)
    ]
    for number in range(3):
        for b in (0, 1):
            entry[pl.ds((2 * number + b) * 8, 8), :] = enters[number][b]


def own_kernel(lines, entry, own, kept):
    enters = [[entry[pl.ds((2 * number + b) * 8, 8), :] for b in (0, 1)] for number in range(3)]
    apply_map(lines, own, enters, kept)


def part_copy(half, position, value, out, sem):
    lanes = pl.ds(pl.multiple_of(position * half, half), half)
    return pltpu.make_async_copy(value, out.at[0, :, :, :, lanes], sem)


def store_kernel(half, kept, out, sem):
    one = part_copy(half, half_of(), kept, out, sem.at[0])
    one.start()
    one.wait()


def last_kernel(lines, half, entry, away, before, out, value, sem):
    own_kernel(lines, entry, away, value)
    one = part_copy(half, 1 - half_of(), value.reshape(lines, value.shape[0] // (2 * lines), 2, half), out, sem.at[0])
    one.start()
    one.wait()


def per_device(krylov, inverse, back, front, left, right):
    _, lines, vectors, _, cells = krylov.shape
    count = lax.axis_size("gy")
    levels = count.bit_length() - 1
    half = cells // 2
    width = vectors + 2 * UNITS
    assert lax.axis_size("gx") == 2 and count == 1 << levels and levels > 1
    assert vectors == 8 and half == 128
    swap = [(0, 1), (1, 0)]

    arguments = [pltpu.with_memory_space_constraint(x, pltpu.HBM) for x in (krylov, inverse, back, front, left, right)]

    def pack(away):
        (out,) = call(
            functools.partial(pack_kernel, half, vectors, away),
            [(lines, vectors + 8, 2, half)],
            arguments,
            [pltpu.SemaphoreType.DMA((5,))],
            specs=[HBM] * 6,
        )
        return out.reshape(-1, half)

    recv = lax.ppermute(pack(True), "gx", swap)
    keep = pack(False)
    swept, early, own_maps = call(
        functools.partial(early_kernel, lines, vectors),
        [(2 * lines * width, half), (ROWS, half), (12 * lines, half)],
        (keep,),
    )
    edge, fixed, second, late = call(
        functools.partial(local_kernel, lines, vectors),
        [(ROWS, half), (2 * lines * width, half), (2 * lines * width, half), (2 * lines * width, half)],
        (keep, recv, swept, early, own_maps),
        [pltpu.VMEM((12 * lines, half), jnp.float32)],
    )
    mids = []
    for level in range(levels - 1):
        got = lax.ppermute(edge, "gy", [(j, j ^ (1 << level)) for j in range(count)])
        last = level == levels - 2
        edge, mid = call(
            functools.partial(merge_kernel, 1 << level, last),
            [(LAST_ROWS if last else ROWS, half), (ROWS, half)],
            (edge, got),
            [pltpu.VMEM((LAST_UNITS, half), jnp.float32)] * (2 * last),
        )
        mids.append(mid)
    across = [(core * count + j, (1 - core) * count + (j ^ (count // 2))) for core in (0, 1) for j in range(count)]
    got = lax.ppermute(edge, ("gx", "gy"), across)
    own, away = call(
        functools.partial(compose_kernel, lines, levels),
        [(2 * lines * width, half)] * 2,
        (*mids, fixed, second, swept, late),
        [pltpu.VMEM((2 * lines * width, half), jnp.float32)] * 2,
    )
    away = lax.ppermute(away, "gx", swap)
    (entry,) = call(
        functools.partial(finish_kernel, levels),
        [(VECTOR_ROWS // 2, half)],
        (edge, got),
        [pltpu.VMEM((LAST_ROWS, half), jnp.float32)] * 2,
    )
    got_entry = lax.ppermute(entry, "gx", swap)

    def plane_half(carries, ref):
        (value,) = call(functools.partial(own_kernel, lines), [(lines * 16, half)], (carries, ref))
        return value.reshape(lines, vectors, 2, half)

    kept = plane_half(entry, own)
    (out,) = call(
        functools.partial(store_kernel, half),
        [krylov.shape],
        [kept],
        [pltpu.SemaphoreType.DMA((1,))],
        specs=[ANY],
        out_specs=[HBM],
    )
    (out,) = call(
        functools.partial(last_kernel, lines, half),
        [krylov.shape],
        [got_entry, away, out],
        [pltpu.VMEM((lines * 16, half), jnp.float32), pltpu.SemaphoreType.DMA((1,))],
        specs=[VMEM, VMEM, HBM],
        out_specs=[HBM],
        aliases={2: 0},
    )
    return out


def solution(mesh):
    spec = P("gx", "gy", None, None, None)
    return jax.shard_map(
        per_device, mesh=mesh, in_specs=(spec,) * 6, out_specs=spec, check_vma=False
    )
```
